256 devices in a mesh: row: 32 (over y_hi, z, core), col: 8 (over y_lo, x).
Axes of the slice: x: 4, y: 4 (y_hi: 2, y_lo: 2; y = y_hi * 2 + y_lo), z: 8, core: 2. Of those that a mesh axis runs over, the one named last changes fastest.
Arguments:
- features: bfloat16 [128, 32768], P(None, ('row', 'col')), may hold values from -6 to 6
- positions: float32 [3, 32768], P(None, ('row', 'col')), may hold values from 0 to 6
- tile_pairs: int32 [32, 8, 2, 4], P('row', 'col'), may hold values from 0 to 31, as said below
- pair_count: int32 [32, 8], P('row', 'col'), may hold values from 1 to 4, as said below
- masks: int32 [32, 8, 4, 128, 128], P('row', 'col'), may hold values 0 or 1
- w_in: bfloat16 [128, 128], replicated, may hold values from -0.5 to 0.5
- w_f1: bfloat16 [64, 128], replicated, may hold values from -3 to 3
- b_f1: float32 [128], replicated, may hold values from -3 to 3
- w_f2: bfloat16 [128, 128], replicated, may hold values from -0.1875 to 0.1875
- b_f2: float32 [128], replicated, may hold values from -2 to 2
- w_o1: bfloat16 [128, 128], replicated, may hold values from -0.25 to 0.25
- b_o1: float32 [128], replicated, may hold values from -3 to 3
- w_o2: bfloat16 [128, 128], replicated, may hold values from -0.5 to 0.5
- b_o2: float32 [128], replicated, may hold values from -3 to 3
- read_w: float32 [128], replicated, may hold values from -2 to 2
Outputs:
- features_out: bfloat16 [128, 32768], P(None, ('row', 'col'))
- forces: float32 [3, 32768], P(None, ('row', 'col'))
The draws below stay inside these ranges and needn't reach their ends.
Inputs may be any that keep to these rules, and one draw needn't show every extreme that they name: Only slots 0 to pair_count[r, c] - 1 of tile_pairs and masks of block (r, c) are listed. tile_pairs[r, c, 0, s] is a receiver tile below 8, tile_pairs[r, c, 1, s] a sender tile below 32; the slots of one grid block hold distinct tile pairs.
All inputs are finite; a program needn't handle non-finite values. No bound on the sum of `masks` on one device may be relied on, other than what follows from the above.
Results may differ from the reference program's by a relative error of at most 0.0075.
Values may be sent and summed in bfloat16 or wider, within the bound.
A program may use at most 64 MiB of HBM per device.

```python
import math
import jax
import jax.numpy as jnp
from jax import lax

F = 128
NB = 64
FH = 128
TILE = 128
TP_MAX = 4
ATOM_DEV = 128
ATOMS = 32768
ROW_BLOCK = 1024
N_ROW = 32
N_COL = 8


def draw_pair_count(key, part):
    key_light, key_busy, key_chosen = jax.random.split(key, 3)
    device_total = N_ROW * N_COL
    light_counts = jax.random.randint(key_light, (device_total,), 1, TP_MAX // 2 + 1)
    busy_draw = jax.random.randint(key_busy, (device_total,), 0, 8)
    counts = jnp.where(busy_draw == 0, TP_MAX, light_counts)
    chosen = jax.random.randint(key_chosen, (), 0, device_total)
    counts = counts.at[chosen].set(TP_MAX)
    return counts.reshape(N_ROW, N_COL).astype(jnp.int32)


def draw_tile_pairs(key, part):
    row_tiles = N_COL * ATOM_DEV // TILE
    col_tiles = N_ROW * ATOM_DEV // TILE
    device_keys = jax.random.split(key, N_ROW * N_COL)

    def choose(one_key):
        return jax.random.permutation(one_key, row_tiles * col_tiles)[:TP_MAX]
    picks = jax.vmap(choose)(device_keys)
    stacked = jnp.stack([picks // col_tiles, picks % col_tiles], axis=1)
    return stacked.reshape(N_ROW, N_COL, 2, TP_MAX).astype(jnp.int32)


def set_ends(entries, rng, low, top_value):
    longest = entries.shape.index(max(entries.shape))
    spots = []
    for shift in (0, 1):
        where = [jax.random.randint(jax.random.fold_in(rng, axis), (), 0, length) for axis, length in enumerate(entries.shape)]
        where[longest] = (where[longest] + shift) % entries.shape[longest]
        spots.append(tuple(where))
    return entries.at[spots[0]].set(low).at[spots[1]].set(top_value)


def levels(own_key, shape, pieces, smallest, largest):
    level, own = 1.0, jax.random.fold_in(own_key, 6)
    for axis_at, blocks in pieces:
        steps = jnp.exp(jax.random.uniform(jax.random.fold_in(own, axis_at), (blocks,), jnp.float32, smallest / len(pieces), largest / len(pieces)))
        level = level * jnp.repeat(steps, shape[axis_at] // blocks).reshape([-1 if axis == axis_at else 1 for axis in range(len(shape))])
    return level


def scatter_about(own_key, shape, deviation, reach, cuts=(), kind=jnp.bfloat16):
    drawn = jax.random.normal(own_key, shape, jnp.float32) * deviation
    if len(cuts) > 0:
        drawn = levels(own_key, shape, cuts, -0.22, 0.18) * drawn
    return jnp.clip(drawn, min=-reach, max=reach).astype(kind)


def setup_inputs(seed: int = 0) -> dict:
    keys = jax.random.split(jax.random.key(seed), 16)
    features = scatter_about(keys[0], (F, ATOMS), 1.0, 6.0, ((1, 256),))
    positions = jnp.clip(6.0 * jax.random.uniform(keys[1], (3, ATOMS), jnp.float32) ** levels(keys[1], (3, ATOMS), ((1, 256),), -0.2, 0.2), 0.0, 6.0)
    tile_pairs = draw_tile_pairs(jax.random.fold_in(keys[15], 71), 0)
    pair_count = draw_pair_count(jax.random.fold_in(keys[15], 71), 0)
    masks = set_ends((jax.random.randint(keys[4], (N_ROW, N_COL, TP_MAX, TILE, TILE), 0, 4) < 3).astype(jnp.int32), jax.random.fold_in(keys[4], 1), 0, 1)
    w_in = scatter_about(keys[5], (F, F), F ** -0.5, 0.5)
    w_f1 = scatter_about(keys[6], (NB, FH), 4 ** -0.5, 3.0)
    b_f1 = scatter_about(keys[7], (FH,), 0.5, 3.0, (), jnp.float32)
    w_f2 = scatter_about(keys[8], (FH, F), (8 * FH) ** -0.5, 0.1875)
    b_f2 = scatter_about(keys[9], (F,), 0.3, 2.0, (), jnp.float32)
    w_o1 = scatter_about(keys[10], (F, F), (4 * F) ** -0.5, 0.25)
    b_o1 = scatter_about(keys[11], (F,), 0.5, 3.0, (), jnp.float32)
    w_o2 = scatter_about(keys[12], (F, F), F ** -0.5, 0.5)
    b_o2 = scatter_about(keys[13], (F,), 0.5, 3.0, (), jnp.float32)
    read_w = scatter_about(keys[14], (F,), 0.3, 2.0, (), jnp.float32)
    return {"features": features, "positions": positions, "tile_pairs": tile_pairs, "pair_count": pair_count, "masks": masks, "w_in": w_in, "w_f1": w_f1, "b_f1": b_f1, "w_f2": w_f2, "b_f2": b_f2, "w_o1": w_o1, "b_o1": b_o1, "w_o2": w_o2, "b_o2": b_o2, "read_w": read_w}


SOFTENING = 0.25
GAMMA_RBF = 10.0
CENTER_MAX = 10.0
CUTOFF = 12.0

def shifted_softplus(value):
    return jax.nn.softplus(value) - math.log(2.0)

def einsum_wide(form, left, right):
    return jnp.einsum(form, left.astype(jnp.float32), right.astype(jnp.float32))

def filter_forward(distance, w_f1, b_f1, w_f2, b_f2):
    nbasis = w_f1.shape[0]
    centers = (jnp.arange(nbasis, dtype=jnp.float32) * (CENTER_MAX / (nbasis - 1)))[:, None, None]
    offset = distance[None] - centers
    gauss = jnp.exp(-GAMMA_RBF * offset * offset)
    basis = gauss.astype(jnp.bfloat16)
    hidden_pre = einsum_wide('kh,krc->hrc', w_f1, basis) + b_f1[:, None, None]
    hidden = shifted_softplus(hidden_pre).astype(jnp.bfloat16)
    filter_base = einsum_wide('hf,hrc->frc', w_f2, hidden) + b_f2[:, None, None]
    cutoff = 0.5 * (jnp.cos(math.pi / CUTOFF * distance) + 1.0)
    return (offset, gauss, hidden_pre, filter_base, cutoff)

def pair_geometry(pos_rows, pos_cols):
    separation = pos_rows[:, :, None] - pos_cols[:, None, :]
    distance = jnp.sqrt(lax.optimization_barrier(jnp.sum(separation * separation, axis=0)) + SOFTENING)
    return (separation, distance)

def block_messages(pos_rows, pos_cols, sender_feats, pair_mask, params):
    separation, distance = pair_geometry(pos_rows, pos_cols)
    offset, gauss, hidden_pre, filter_base, cutoff = filter_forward(distance, *params)
    weighted = filter_base * (cutoff * pair_mask)[None]
    return lax.optimization_barrier(jnp.sum(weighted * sender_feats.astype(jnp.float32)[:, None, :], axis=2))

def block_forces(pos_rows, pos_cols, sender_feats, grad_rows, pair_mask, params):
    w_f1, b_f1, w_f2, b_f2 = params
    separation, distance = pair_geometry(pos_rows, pos_cols)
    offset, gauss, hidden_pre, filter_base, cutoff = filter_forward(distance, *params)
    pair_grad = grad_rows[:, :, None] * sender_feats.astype(jnp.float32)[:, None, :] * pair_mask[None]
    filter_grad = (pair_grad * cutoff[None]).astype(jnp.bfloat16)
    cutoff_grad = lax.optimization_barrier(jnp.sum(pair_grad * filter_base, axis=0))
    hidden_grad = einsum_wide('hf,frc->hrc', w_f2, filter_grad)
    hidden_grad = (hidden_grad * jax.nn.sigmoid(hidden_pre)).astype(jnp.bfloat16)
    basis_grad = einsum_wide('kh,hrc->krc', w_f1, hidden_grad)
    dist_grad = -2.0 * GAMMA_RBF * lax.optimization_barrier(jnp.sum(basis_grad * gauss * offset, axis=0))
    dist_grad = dist_grad - 0.5 * math.pi / CUTOFF * jnp.sin(math.pi / CUTOFF * distance) * cutoff_grad
    push = separation * (dist_grad / distance)[None]
    return (-lax.optimization_barrier(jnp.sum(push, axis=2)), lax.optimization_barrier(jnp.sum(push, axis=1)))

def tile_messages(pos_rows, pos_cols, sender_feats, pair_mask, params):
    rows = pos_rows.shape[1]
    block_rows = min(8, rows)
    block_count = rows // block_rows

    def per_block(block_index):
        start = block_index * block_rows
        return block_messages(lax.dynamic_slice_in_dim(pos_rows, start, block_rows, 1), pos_cols, sender_feats, lax.dynamic_slice_in_dim(pair_mask, start, block_rows, 0), params)
    parts = lax.map(per_block, jnp.arange(block_count, dtype=jnp.int32))
    return jnp.transpose(parts, (1, 0, 2)).reshape(parts.shape[1], rows)

def tile_forces(pos_rows, pos_cols, sender_feats, grad_rows, pair_mask, params):
    rows = pos_rows.shape[1]
    block_rows = min(8, rows)
    block_count = rows // block_rows

    def per_block(block_index):
        start = block_index * block_rows
        return block_forces(lax.dynamic_slice_in_dim(pos_rows, start, block_rows, 1), pos_cols, sender_feats, lax.dynamic_slice_in_dim(grad_rows, start, block_rows, 1), lax.dynamic_slice_in_dim(pair_mask, start, block_rows, 0), params)
    row_parts, col_parts = lax.map(per_block, jnp.arange(block_count, dtype=jnp.int32))
    return (jnp.transpose(row_parts, (1, 0, 2)).reshape(3, rows), lax.optimization_barrier(jnp.sum(col_parts, axis=0)))

def reference(features, positions, tile_pairs, pair_count, masks, w_in, w_f1, b_f1, w_f2, b_f2, w_o1, b_o1, w_o2, b_o2, read_w):
    params = (w_f1, b_f1, w_f2, b_f2)
    projected = einsum_wide('fo,fa->oa', w_in, features).astype(jnp.bfloat16)

    def locate(device_index, slot_index):
        row_index = device_index // N_COL
        col_index = device_index % N_COL
        row_tile = tile_pairs[row_index, col_index, 0, slot_index]
        col_tile = tile_pairs[row_index, col_index, 1, slot_index]
        row_start = row_index * ROW_BLOCK + row_tile * TILE
        local = col_tile * TILE
        col_start = (local // ATOM_DEV * N_COL + col_index) * ATOM_DEV + local % ATOM_DEV
        pair_mask = masks[row_index, col_index, slot_index].astype(jnp.float32)
        return (row_start.astype(jnp.int32), col_start.astype(jnp.int32), pair_mask)

    def count_of(device_index):
        return pair_count[device_index // N_COL, device_index % N_COL]

    def forward_device(totals, device_index):

        def per_slot(slot_index, inner):
            row_start, col_start, pair_mask = locate(device_index, slot_index)
            pos_rows = lax.dynamic_slice_in_dim(positions, row_start, TILE, 1)
            pos_cols = lax.dynamic_slice_in_dim(positions, col_start, TILE, 1)
            sender_feats = lax.dynamic_slice_in_dim(projected, col_start, TILE, 1)
            tile_sum = tile_messages(pos_rows, pos_cols, sender_feats, pair_mask, params)
            current = lax.dynamic_slice_in_dim(inner, row_start, TILE, 1)
            return lax.dynamic_update_slice_in_dim(inner, current + tile_sum, row_start, 1)
        return (lax.fori_loop(jnp.int32(0), count_of(device_index), per_slot, totals), None)
    device_ids = jnp.arange(N_ROW * N_COL, dtype=jnp.int32)
    messages, _ = lax.scan(forward_device, jnp.zeros((F, ATOMS), jnp.float32), device_ids)
    pre_act = einsum_wide('fo,fa->oa', w_o1, messages.astype(jnp.bfloat16)) + b_o1[:, None]
    activated = shifted_softplus(pre_act).astype(jnp.bfloat16)
    update = einsum_wide('fo,fa->oa', w_o2, activated) + b_o2[:, None]
    features_out = (features.astype(jnp.float32) + update).astype(jnp.bfloat16)
    direction = jnp.dot(w_o2.astype(jnp.float32), read_w, precision=lax.Precision.HIGHEST)
    message_grad = jnp.dot(w_o1.astype(jnp.float32), direction[:, None] * jax.nn.sigmoid(pre_act), precision=lax.Precision.HIGHEST)

    def backward_device(totals, device_index):

        def per_slot(slot_index, inner):
            row_start, col_start, pair_mask = locate(device_index, slot_index)
            pos_rows = lax.dynamic_slice_in_dim(positions, row_start, TILE, 1)
            pos_cols = lax.dynamic_slice_in_dim(positions, col_start, TILE, 1)
            sender_feats = lax.dynamic_slice_in_dim(projected, col_start, TILE, 1)
            grad_rows = lax.dynamic_slice_in_dim(message_grad, row_start, TILE, 1)
            row_part, col_part = tile_forces(pos_rows, pos_cols, sender_feats, grad_rows, pair_mask, params)
            current = lax.dynamic_slice_in_dim(inner, row_start, TILE, 1)
            inner = lax.dynamic_update_slice_in_dim(inner, current + row_part, row_start, 1)
            current = lax.dynamic_slice_in_dim(inner, col_start, TILE, 1)
            return lax.dynamic_update_slice_in_dim(inner, current + col_part, col_start, 1)
        return (lax.fori_loop(jnp.int32(0), count_of(device_index), per_slot, totals), None)
    forces, _ = lax.scan(backward_device, jnp.zeros((3, ATOMS), jnp.float32), device_ids)
    return (features_out, forces)
```

```python
import functools
import math

import jax
import jax.numpy as jnp
from jax import lax
from jax.experimental import pallas as pl
from jax.experimental.pallas import tpu as pltpu
from jax.sharding import PartitionSpec as P

SOFTENING = 0.25
GAMMA_RBF = 10.0
CENTER_MAX = 10.0
CUTOFF = 12.0
LN2 = math.log(2.0)
SCALE = math.sqrt(GAMMA_RBF / LN2)
F32 = jnp.float32
BF16 = jnp.bfloat16
MESH = pl.DeviceIdType.MESH


def cos_sin(x):
    y = x * x
    cos_acc = jnp.full_like(y, 1.0 / math.factorial(14)) * -1.0
    for n in (12, 10, 8, 6, 4, 2, 0):
        sign = 1.0 if (n // 2) % 2 == 0 else -1.0
        cos_acc = cos_acc * y + sign / math.factorial(n)
    sin_acc = jnp.full_like(y, 1.0 / math.factorial(13))
    for n in (11, 9, 7, 5, 3, 1):
        sign = 1.0 if ((n - 1) // 2) % 2 == 0 else -1.0
        sin_acc = sin_acc * y + sign / math.factorial(n)
    return cos_acc, sin_acc * x


def pieces(value):
    high = value.astype(BF16)
    rest = value - high.astype(F32)
    mid = rest.astype(BF16)
    low = (rest - mid.astype(F32)).astype(BF16)
    return high, mid, low


def row16(row):
    block = jnp.broadcast_to(row, (16, row.shape[1])).astype(BF16)
    return jnp.concatenate([block] * 8, axis=0)


def kernel(
    n_row, n_col, n_slot,
    pairs_ref, count_ref, feat_ref, pos_ref, mask_ref,
    w_in_ref, w1_ref, b1_ref, w2_ref, b2_ref, wo1_ref, bo1_ref, wo2_ref, bo2_ref, rw_ref,
    fout_ref, force_ref,
    pos_row, pos_col, proj_own, proj_all,
    w1a, w2f, diag,
    dist, cm, cpm, unit,
    hid, msg, part, msg_in, grad_own, grad_all, grad_f, dgrad,
    rforce, cforce, rpart, cpart, rforce_in, cforce_in,
    prs, prr, pcs, pcr, js, jr, ms, mr, gs, gr, rfs, rfr, cfs, cfr,
):
    my_row = lax.axis_index("row")
    my_col = lax.axis_index("col")
    half = 64

    def row_peer(k):
        return lax.rem(my_row + k, n_row)

    def col_peer(k):
        return lax.rem(my_col + k, n_col)

    def to_row(src, dst, ssem, rsem, peer):
        return pltpu.make_async_remote_copy(
            src_ref=src, dst_ref=dst, send_sem=ssem, recv_sem=rsem,
            device_id={"row": peer}, device_id_type=MESH,
        )

    def to_col(src, dst, ssem, rsem, peer):
        return pltpu.make_async_remote_copy(
            src_ref=src, dst_ref=dst, send_sem=ssem, recv_sem=rsem,
            device_id={"col": peer}, device_id_type=MESH,
        )

    def each(n, body):
        def step(k, carry):
            body(k)
            return carry
        lax.fori_loop(1, n, step, 0)

    barrier = pltpu.get_barrier_semaphore()
    each(n_row, lambda k: pl.semaphore_signal(
        barrier, inc=1, device_id={"row": row_peer(k)}, device_id_type=MESH))
    each(n_col, lambda k: pl.semaphore_signal(
        barrier, inc=1, device_id={"col": col_peer(k)}, device_id_type=MESH))

    feat_t = jnp.transpose(feat_ref[...].astype(F32))
    proj_own[...] = jnp.dot(
        feat_t.astype(BF16), w_in_ref[...], preferred_element_type=F32
    ).astype(BF16)
    proj_all[my_row] = proj_own[...]
    pos_row[my_col] = pos_ref[...]
    pos_col[my_row] = pos_ref[...]

    bias = jnp.transpose(jnp.broadcast_to(b1_ref[...] - LN2, (128, 128)))
    high, mid, low = pieces(bias)
    lane = lax.broadcasted_iota(jnp.int32, (128, 128), 1)
    zero = jnp.zeros((128, 128), F32)
    extra = jnp.where(lane == 64, high.astype(F32), zero)
    extra = jnp.where(lane == 65, mid.astype(F32), extra)
    extra = jnp.where(lane == 66, low.astype(F32), extra)
    w1t = jnp.transpose(
        jnp.concatenate([w1_ref[...].astype(F32), jnp.zeros((64, 128), F32)], axis=0)
    )
    w1a[...] = (w1t + extra).astype(BF16)
    w2f[...] = w2_ref[...].astype(F32)
    diag[...] = jnp.zeros_like(diag)

    pl.semaphore_wait(barrier, n_row - 1 + n_col - 1)

    def pos_row_copy(k, src_index):
        return to_col(pos_ref, pos_row.at[src_index], pcs.at[k], pcr.at[src_index], col_peer(k))

    def pos_col_copy(k, src_index):
        return to_row(pos_ref, pos_col.at[src_index], prs.at[k], prr.at[src_index], row_peer(k))

    def proj_copy(k, src_index):
        return to_row(proj_own, proj_all.at[src_index], js.at[k], jr.at[src_index], row_peer(k))

    each(n_row, lambda k: pos_col_copy(k, my_row).start())
    each(n_col, lambda k: pos_row_copy(k, my_col).start())
    each(n_row, lambda k: proj_copy(k, my_row).start())
    each(n_row, lambda k: pos_col_copy(k, row_peer(k)).wait_recv())
    each(n_col, lambda k: pos_row_copy(k, col_peer(k)).wait_recv())

    def tiles_of(s):
        t = jnp.clip(pairs_ref[0, s], 0, n_col - 1)
        c = jnp.clip(pairs_ref[1, s], 0, n_row - 1)
        return t, c

    def geometry(s, carry):
        t, c = tiles_of(s)
        pr = pos_row[t]
        pc = pos_col[c]
        seps = []
        d2 = None
        for a in range(3):
            column = jnp.transpose(jnp.broadcast_to(pr[a:a + 1, :], (128, 128)))
            sep = column - pc[a:a + 1, :]
            seps.append(sep)
            d2 = sep * sep if d2 is None else d2 + sep * sep
        d2 = d2 + SOFTENING
        d = jnp.sqrt(d2)
        inv = 1.0 / d
        cos_h, sin_h = cos_sin(d * (0.5 * math.pi / CUTOFF))
        listed = jnp.where(s < count_ref[0, 0], 1.0, 0.0)
        m = mask_ref[s].astype(F32) * listed
        dist[s] = d * SCALE
        cm[s] = m * (cos_h * cos_h)
        cpm[s] = m * ((-math.pi / CUTOFF) * (sin_h * cos_h))
        for a in range(3):
            unit[s, a] = seps[a] * inv
        return carry

    lax.fori_loop(0, n_slot, geometry, 0)

    mu = lax.broadcasted_iota(jnp.int32, (64, 128), 0).astype(F32) * (
        CENTER_MAX / 63.0 * SCALE
    )
    ones = jnp.ones((16, 256), BF16)

    def rows_of(ref, s, ip):
        return ref[s, pl.ds(ip, 1), :], ref[s, pl.ds(ip + half, 1), :]

    def set_diag(c):
        p = proj_all[c]
        diag[0:128, 0:128] = p
        diag[128:256, 128:256] = p

    each(n_row, lambda k: proj_copy(k, row_peer(k)).wait_recv())

    def forward_slot(s, carry):
        t, c = tiles_of(s)
        set_diag(c)

        def step(ip, inner):
            d1, d2 = rows_of(dist, s, ip)
            x1 = d1 - mu
            x2 = d2 - mu
            g = jnp.concatenate(
                [jnp.exp2(-(x1 * x1)).astype(BF16), jnp.exp2(-(x2 * x2)).astype(BF16)], axis=1
            )
            rhs = jnp.concatenate([g, ones], axis=0)
            pre = jnp.dot(w1a[:, 0:80], rhs, preferred_element_type=F32)
            hidden = jnp.log(jnp.exp(pre) + 0.5).astype(BF16)
            hid[s, ip] = hidden
            c1, c2 = rows_of(cm, s, ip)
            scaled = hidden * row16(jnp.concatenate([c1, c2], axis=1))
            a = jnp.dot(scaled, diag[...], preferred_element_type=F32)
            w2 = w2f[...]
            msg[s, pl.ds(ip, 1), :] = jnp.sum(a[:, 0:128] * w2, axis=0, keepdims=True)
            msg[s, pl.ds(ip + half, 1), :] = jnp.sum(a[:, 128:256] * w2, axis=0, keepdims=True)
            return inner

        lax.fori_loop(0, half, step, 0)
        weight_sum = jnp.dot(
            cm[s].astype(BF16), diag[0:128, 0:128], preferred_element_type=F32
        )
        msg[s] = msg[s] + weight_sum * b2_ref[...]
        return carry

    lax.fori_loop(0, n_slot, forward_slot, 0)

    def gather_tile(tile, carry):
        total = None
        for s in range(n_slot):
            t, _ = tiles_of(s)
            term = msg[s] * jnp.where(t == tile, 1.0, 0.0)
            total = term if total is None else total + term
        part[tile] = total.astype(BF16)
        return carry

    lax.fori_loop(0, n_col, gather_tile, 0)
    msg_in[my_col] = part[my_col]

    def msg_copy(k, tile, src_index):
        return to_col(part.at[tile], msg_in.at[src_index], ms.at[k], mr.at[src_index], col_peer(k))

    each(n_col, lambda k: msg_copy(k, col_peer(k), my_col).start())

    def derivative_slot(s, carry):
        def step(ip, inner):
            d1, d2 = rows_of(dist, s, ip)
            x1 = d1 - mu
            x2 = d2 - mu
            factor = -2.0 * GAMMA_RBF / SCALE
            g1 = jnp.exp2(-(x1 * x1)) * (x1 * factor)
            g2 = jnp.exp2(-(x2 * x2)) * (x2 * factor)
            g = jnp.concatenate([g1.astype(BF16), g2.astype(BF16)], axis=1)
            slope = jnp.dot(w1a[:, 0:64], g, preferred_element_type=F32)
            hidden = hid[s, ip].astype(F32)
            sig = 1.0 - 0.5 * jnp.exp(-hidden)
            c1, c2 = rows_of(cm, s, ip)
            e1, e2 = rows_of(cpm, s, ip)
            c_row = jnp.concatenate([c1, c2], axis=1)
            e_row = jnp.concatenate([e1, e2], axis=1)
            hid[s, ip] = (slope * (sig * c_row) + hidden * e_row).astype(BF16)
            return inner

        lax.fori_loop(0, half, step, 0)
        return carry

    lax.fori_loop(0, n_slot, derivative_slot, 0)

    each(n_col, lambda k: msg_copy(k, col_peer(k), col_peer(k)).wait_recv())
    total = msg_in[0].astype(F32)
    for k in range(1, n_col):
        total = total + msg_in[k].astype(F32)
    pre = jnp.dot(total.astype(BF16), wo1_ref[...], preferred_element_type=F32) + bo1_ref[...]
    small = jnp.exp(-jnp.abs(pre))
    activated = (jnp.maximum(pre, 0.0) + jnp.log(1.0 + small) - LN2).astype(BF16)
    sig = jnp.where(pre >= 0.0, 1.0, small) / (1.0 + small)
    direction = lax.dot_general(
        jnp.broadcast_to(rw_ref[...], (8, 128)), wo2_ref[...].astype(F32),
        (((1,), (1,)), ((), ())), precision=lax.Precision.HIGHEST,
        preferred_element_type=F32,
    )[0:1, :]
    grad_own[...] = lax.dot_general(
        sig * direction, wo1_ref[...].astype(F32), (((1,), (1,)), ((), ())),
        precision=lax.Precision.HIGHEST, preferred_element_type=F32,
    ).astype(BF16)
    grad_all[my_col] = grad_own[...]

    def grad_copy(k, src_index):
        return to_col(grad_own, grad_all.at[src_index], gs.at[k], gr.at[src_index], col_peer(k))

    each(n_col, lambda k: grad_copy(k, my_col).start())
    update = jnp.dot(activated, wo2_ref[...], preferred_element_type=F32) + bo2_ref[...]
    fout_ref[...] = (feat_ref[...].astype(F32) + jnp.transpose(update)).astype(BF16)
    each(n_col, lambda k: grad_copy(k, col_peer(k)).wait_recv())

    def force_slot(s, carry):
        t, c = tiles_of(s)
        set_diag(c)
        grad_f[...] = grad_all[t].astype(F32)

        def step(ip, inner):
            r1 = grad_f[pl.ds(ip, 1), :]
            r2 = grad_f[pl.ds(ip + half, 1), :]
            w2 = w2_ref[...]
            lhs = jnp.concatenate([w2 * row16(r1), w2 * row16(r2)], axis=1)
            q = lax.dot_general(
                lhs, diag[...], (((1,), (1,)), ((), ())), preferred_element_type=F32
            )
            row = jnp.sum(q * hid[s, ip].astype(F32), axis=0, keepdims=True)
            dgrad[pl.ds(ip, 1), :] = row[:, 0:128]
            dgrad[pl.ds(ip + half, 1), :] = row[:, 128:256]
            return inner

        lax.fori_loop(0, half, step, 0)
        g_b2 = (grad_f[...] * b2_ref[...]).astype(BF16)
        plain = lax.dot_general(
            g_b2, diag[0:128, 0:128], (((1,), (1,)), ((), ())), preferred_element_type=F32
        )
        d = dgrad[...] + cpm[s] * plain
        rows, cols = [], []
        for a in range(3):
            push = unit[s, a] * d
            cols.append(jnp.sum(push, axis=0, keepdims=True))
            rows.append(-jnp.sum(jnp.transpose(push), axis=0, keepdims=True))
        pad = [jnp.zeros((5, 128), F32)]
        rforce[s] = jnp.concatenate(rows + pad, axis=0)
        cforce[s] = jnp.concatenate(cols + pad, axis=0)
        return carry

    lax.fori_loop(0, n_slot, force_slot, 0)

    def spread(source, target, which, n):
        def one(tile, carry):
            total = None
            for s in range(n_slot):
                term = source[s] * jnp.where(tiles_of(s)[which] == tile, 1.0, 0.0)
                total = term if total is None else total + term
            target[tile] = total
            return carry
        lax.fori_loop(0, n, one, 0)

    spread(cforce, cpart, 1, n_row)
    spread(rforce, rpart, 0, n_col)
    cforce_in[my_row] = cpart[my_row]
    rforce_in[my_col] = rpart[my_col]

    def cforce_copy(k, tile, src_index):
        return to_row(cpart.at[tile], cforce_in.at[src_index], cfs.at[k], cfr.at[src_index], row_peer(k))

    def rforce_copy(k, tile, src_index):
        return to_col(rpart.at[tile], rforce_in.at[src_index], rfs.at[k], rfr.at[src_index], col_peer(k))

    each(n_row, lambda k: cforce_copy(k, row_peer(k), my_row).start())
    each(n_col, lambda k: rforce_copy(k, col_peer(k), my_col).start())

    each(n_row, lambda k: pos_col_copy(k, my_row).wait_send())
    each(n_col, lambda k: pos_row_copy(k, my_col).wait_send())
    each(n_row, lambda k: proj_copy(k, my_row).wait_send())
    each(n_col, lambda k: msg_copy(k, col_peer(k), my_col).wait_send())
    each(n_col, lambda k: grad_copy(k, my_col).wait_send())

    each(n_col, lambda k: rforce_copy(k, col_peer(k), col_peer(k)).wait_recv())
    each(n_row, lambda k: cforce_copy(k, row_peer(k), row_peer(k)).wait_recv())
    force = rforce_in[0]
    for k in range(1, n_col):
        force = force + rforce_in[k]
    for k in range(n_row):
        force = force + cforce_in[k]
    force_ref[...] = force[0:3, :]
    each(n_row, lambda k: cforce_copy(k, row_peer(k), my_row).wait_send())
    each(n_col, lambda k: rforce_copy(k, col_peer(k), my_col).wait_send())


def solution(mesh):
    n_row, n_col = mesh.shape["row"], mesh.shape["col"]

    def local(features, positions, tile_pairs, pair_count, masks, w_in, w_f1, b_f1, w_f2, b_f2,
              w_o1, b_o1, w_o2, b_o2, read_w):
        n_slot = masks.shape[2]
        vmem = pl.BlockSpec(memory_space=pltpu.VMEM)
        smem = pl.BlockSpec(memory_space=pltpu.SMEM)
        tile = (128, 128)
        dma = pltpu.SemaphoreType.DMA
        return pl.pallas_call(
            functools.partial(kernel, n_row, n_col, n_slot),
            out_shape=(
                jax.ShapeDtypeStruct(features.shape, BF16),
                jax.ShapeDtypeStruct(positions.shape, F32),
            ),
            in_specs=[smem, smem] + [vmem] * 13,
            out_specs=(vmem, vmem),
            scratch_shapes=[
                pltpu.VMEM((n_col, 3, 128), F32),
                pltpu.VMEM((n_row, 3, 128), F32),
                pltpu.VMEM(tile, BF16),
                pltpu.VMEM((n_row,) + tile, BF16),
                pltpu.VMEM(tile, BF16),
                pltpu.VMEM(tile, F32),
                pltpu.VMEM((256, 256), BF16),
                pltpu.VMEM((n_slot,) + tile, F32),
                pltpu.VMEM((n_slot,) + tile, F32),
                pltpu.VMEM((n_slot,) + tile, F32),
                pltpu.VMEM((n_slot, 3) + tile, F32),
                pltpu.VMEM((n_slot, 64, 128, 256), BF16),
                pltpu.VMEM((n_slot,) + tile, F32),
                pltpu.VMEM((n_col,) + tile, BF16),
                pltpu.VMEM((n_col,) + tile, BF16),
                pltpu.VMEM(tile, BF16),
                pltpu.VMEM((n_col,) + tile, BF16),
                pltpu.VMEM(tile, F32),
                pltpu.VMEM(tile, F32),
                pltpu.VMEM((n_slot, 8, 128), F32),
                pltpu.VMEM((n_slot, 8, 128), F32),
                pltpu.VMEM((n_col, 8, 128), F32),
                pltpu.VMEM((n_row, 8, 128), F32),
                pltpu.VMEM((n_col, 8, 128), F32),
                pltpu.VMEM((n_row, 8, 128), F32),
                dma((n_row,)), dma((n_row,)),
                dma((n_col,)), dma((n_col,)),
                dma((n_row,)), dma((n_row,)),
                dma((n_col,)), dma((n_col,)),
                dma((n_col,)), dma((n_col,)),
                dma((n_col,)), dma((n_col,)),
                dma((n_row,)), dma((n_row,)),
            ],
            compiler_params=pltpu.CompilerParams(
                collective_id=0, has_side_effects=True, vmem_limit_bytes=56 << 20
            ),
        )(
            tile_pairs.reshape(tile_pairs.shape[2:]), pair_count, features, positions,
            masks.reshape(masks.shape[2:]),
            w_in, w_f1, b_f1.reshape(1, -1), w_f2, b_f2.reshape(1, -1),
            w_o1, b_o1.reshape(1, -1), w_o2, b_o2.reshape(1, -1), read_w.reshape(1, -1),
        )

    split = P(None, ("row", "col"))
    return jax.shard_map(
        local, mesh=mesh,
        in_specs=(split, split, P("row", "col", None, None), P("row", "col"),
                  P("row", "col", None, None, None)) + (P(),) * 10,
        out_specs=(split, split), check_vma=False,
    )
```

```python
import functools
import math

import jax
import jax.numpy as jnp
from jax import lax
from jax.experimental import pallas as pl
from jax.experimental.pallas import tpu as pltpu
from jax.sharding import PartitionSpec as P

SOFTENING = 0.25
GAMMA_RBF = 10.0
CENTER_MAX = 10.0
CUTOFF = 12.0
LN2 = math.log(2.0)
SCALE = math.sqrt(GAMMA_RBF / LN2)
SLOPE = -2.0 * GAMMA_RBF / SCALE
F32 = jnp.float32
BF16 = jnp.bfloat16
MESH = pl.DeviceIdType.MESH
PAIRS = 8
HAND = 13
LAG = 15
SPLIT = 16


def cos_sin(x):
    y = x * x
    cos_acc = jnp.full_like(y, 1.0 / math.factorial(14)) * -1.0
    for n in (12, 10, 8, 6, 4, 2, 0):
        sign = 1.0 if (n // 2) % 2 == 0 else -1.0
        cos_acc = cos_acc * y + sign / math.factorial(n)
    sin_acc = jnp.full_like(y, 1.0 / math.factorial(13))
    for n in (11, 9, 7, 5, 3, 1):
        sign = 1.0 if ((n - 1) // 2) % 2 == 0 else -1.0
        sin_acc = sin_acc * y + sign / math.factorial(n)
    return cos_acc, sin_acc * x


def pieces(value):
    high = value.astype(BF16)
    rest = value - high.astype(F32)
    mid = rest.astype(BF16)
    low = (rest - mid.astype(F32)).astype(BF16)
    return high, mid, low


def row16(row):
    block = jnp.broadcast_to(row, (16, row.shape[1])).astype(BF16)
    return jnp.concatenate([block] * 8, axis=0)


def kernel(
    n_row, n_col, n_slot,
    pairs_ref, count_ref, feat_ref, pos_ref, mask_ref,
    w_in_ref, w1_ref, b1_ref, w2_ref, b2_ref, wo1_ref, bo1_ref, wo2_ref, bo2_ref, rw_ref,
    fout_ref, force_ref,
    pos_row, pos_col, proj_all,
    w1a, w1d, w2f, diag, diag_t,
    dist, cm, cpm, ratio, unit,
    hid, slope_in, msg, part, msg_in, grad_own, grad_all, grad_f, dgrad,
    rforce, cforce, rpart, cpart, rforce_in, cforce_in,
    prs, prr, pcs, pcr, js, jh, jr, ms, mr, gs, gr, rfs, rfr, cfs, cfr,
):
    my_row = lax.axis_index("row")
    my_col = lax.axis_index("col")
    half = 64

    def row_peer(k):
        return lax.rem(my_row + k, n_row)

    def col_peer(k):
        return lax.rem(my_col + k, n_col)

    def to_row(src, dst, ssem, rsem, peer):
        return pltpu.make_async_remote_copy(
            src_ref=src, dst_ref=dst, send_sem=ssem, recv_sem=rsem,
            device_id={"row": peer}, device_id_type=MESH,
        )

    def to_col(src, dst, ssem, rsem, peer):
        return pltpu.make_async_remote_copy(
            src_ref=src, dst_ref=dst, send_sem=ssem, recv_sem=rsem,
            device_id={"col": peer}, device_id_type=MESH,
        )

    def each(n, body):
        def step(k, carry):
            body(k)
            return carry
        lax.fori_loop(1, n, step, 0)

    barrier = pltpu.get_barrier_semaphore()
    each(n_row, lambda k: pl.semaphore_signal(
        barrier, inc=1, device_id={"row": row_peer(k)}, device_id_type=MESH))
    each(n_col, lambda k: pl.semaphore_signal(
        barrier, inc=1, device_id={"col": col_peer(k)}, device_id_type=MESH))

    def pos_row_copy(k, src_index):
        return to_col(pos_ref, pos_row.at[src_index], pcs.at[k], pcr.at[src_index], col_peer(k))

    def pos_col_copy(k, src_index):
        return to_row(pos_ref, pos_col.at[src_index], prs.at[k], prr.at[src_index], row_peer(k))

    core = lax.rem(my_row, 2)
    n_chip = n_row // 2

    def chip_peer(k):
        return lax.rem(my_row // 2 + k, n_chip) * 2 + core

    def proj_copy(k, src_index):
        return to_row(
            proj_all.at[my_row], proj_all.at[src_index], js.at[k], jr.at[src_index], chip_peer(k)
        )

    def proj_hand(k):
        return to_row(
            proj_all.at[chip_peer(k)], proj_all.at[chip_peer(k)], jh.at[k], jr.at[chip_peer(k)],
            my_row + 1 - 2 * core,
        )

    def proj_arrival(k):
        src = chip_peer(k) + 1 - 2 * core
        return to_row(
            proj_all.at[src], proj_all.at[src], jh.at[k], jr.at[src], my_row + 1 - 2 * core
        )

    pl.semaphore_wait(barrier, n_row - 1 + n_col - 1)
    each(n_row, lambda k: pos_col_copy(k, my_row).start())
    each(n_col, lambda k: pos_row_copy(k, my_col).start())

    feat_t = jnp.transpose(feat_ref[...].astype(F32))
    proj_all[my_row] = jnp.dot(
        feat_t.astype(BF16), w_in_ref[...], preferred_element_type=F32
    ).astype(BF16)
    each(n_chip, lambda k: proj_copy(k, my_row).start())
    proj_hand(0).start()
    pos_row[my_col] = pos_ref[...]
    pos_col[my_row] = pos_ref[...]

    bias = jnp.transpose(jnp.broadcast_to(b1_ref[...] - LN2, (128, 128)))
    high, mid, low = pieces(bias)
    lane = lax.broadcasted_iota(jnp.int32, (128, 128), 1)
    zero = jnp.zeros((128, 128), F32)
    extra = jnp.where(lane == 64, high.astype(F32), zero)
    extra = jnp.where(lane == 65, mid.astype(F32), extra)
    extra = jnp.where(lane == 66, low.astype(F32), extra)
    w1t = jnp.transpose(
        jnp.concatenate([w1_ref[...].astype(F32), jnp.zeros((64, 128), F32)], axis=0)
    )
    w1a[...] = (w1t + extra).astype(BF16)
    w1d[...] = w1t[:, 0:64].astype(BF16)
    w2f[...] = w2_ref[...].astype(F32)

    each(n_row, lambda k: pos_col_copy(k, row_peer(k)).wait_recv())
    each(n_col, lambda k: pos_row_copy(k, col_peer(k)).wait_recv())

    def tiles_of(s):
        t = jnp.clip(pairs_ref[0, s], 0, n_col - 1)
        c = jnp.clip(pairs_ref[1, s], 0, n_row - 1)
        return t, c

    def geometry(s, carry):
        t, c = tiles_of(s)
        pr = pos_row[t]
        pc = pos_col[c]
        seps = []
        d2 = None
        for a in range(3):
            column = jnp.transpose(jnp.broadcast_to(pr[a:a + 1, :], (128, 128)))
            sep = column - pc[a:a + 1, :]
            seps.append(sep)
            d2 = sep * sep if d2 is None else d2 + sep * sep
        d2 = d2 + SOFTENING
        d = jnp.sqrt(d2)
        inv = 1.0 / d
        cos_h, sin_h = cos_sin(d * (0.5 * math.pi / CUTOFF))
        listed = jnp.where(s < count_ref[0, 0], 1.0, 0.0)
        m = mask_ref[s].astype(F32) * listed
        dist[s] = d * SCALE
        cm[s] = m * (cos_h * cos_h)
        slope_c = (-math.pi / CUTOFF) * sin_h
        cpm[s] = m * (slope_c * cos_h)
        ratio[s] = (LN2 / SLOPE) * (slope_c / cos_h)
        for a in range(3):
            unit[s, a] = seps[a] * inv
        return carry

    lax.fori_loop(0, n_slot, geometry, 0)

    mu = lax.broadcasted_iota(jnp.int32, (64, 128), 0).astype(F32) * (
        CENTER_MAX / 63.0 * SCALE
    )
    ones = jnp.ones((16, 256), BF16)
    groups = half // PAIRS

    def pair_row(ref, s, ip):
        return jnp.concatenate(
            [ref[s, pl.ds(ip, 1), :], ref[s, pl.ds(ip + half, 1), :]], axis=1
        )

    def hidden_group(n):
        s, base = n // groups, lax.rem(n, groups) * PAIRS
        for b in range(PAIRS):
            ip = base + b
            x = jnp.concatenate(
                [dist[s, pl.ds(ip, 1), :] - mu, dist[s, pl.ds(ip + half, 1), :] - mu], axis=1
            )
            wide = jnp.exp2(-(x * x))
            slope_in[s, ip] = (wide * x).astype(BF16)
            g = wide.astype(BF16)
            pre = jnp.dot(
                w1a[:, 0:80], jnp.concatenate([g, ones], axis=0), preferred_element_type=F32
            ).astype(BF16)
            e = jnp.exp2(pre * jnp.asarray(1.0 / LN2, BF16))
            hid[s, ip] = lax.log2(e + jnp.asarray(0.5, BF16))

    def message_group(n):
        s, base = n // groups, lax.rem(n, groups) * PAIRS
        scaled = jnp.concatenate(
            [hid[s, base + b] * row16(pair_row(cm, s, base + b) * LN2) for b in range(PAIRS)],
            axis=0,
        )
        a = jnp.dot(scaled, diag[s], preferred_element_type=F32)
        w2 = w2f[...]
        for b in range(PAIRS):
            part_a = a[b * 128:(b + 1) * 128]
            msg[s, pl.ds(base + b, 1), :] = jnp.sum(part_a[:, 0:128] * w2, axis=0, keepdims=True)
            msg[s, pl.ds(base + b + half, 1), :] = jnp.sum(
                part_a[:, 128:256] * w2, axis=0, keepdims=True
            )

    total_groups = n_slot * groups

    def run(first, last, body):
        def step(n, carry):
            body(n)
            return carry
        lax.fori_loop(first, last, step, 0)

    run(0, HAND, hidden_group)

    def hand_on(k):
        proj_copy(k, chip_peer(k)).wait_recv()
        proj_hand(k).start()

    each(n_chip, hand_on)

    run(HAND, LAG, hidden_group)
    proj_arrival(0).wait_recv()
    each(n_chip, lambda k: proj_arrival(k).wait_recv())

    def set_diag(s, carry):
        _, c = tiles_of(s)
        p = proj_all[c]
        z = jnp.zeros((128, 128), BF16)
        diag[s, 0:128, 0:128] = p
        diag[s, 0:128, 128:256] = z
        diag[s, 128:256, 0:128] = z
        diag[s, 128:256, 128:256] = p
        q = jnp.transpose(p.astype(F32)).astype(BF16)
        diag_t[s, 0:128, 0:128] = q
        diag_t[s, 0:128, 128:256] = z
        diag_t[s, 128:256, 0:128] = z
        diag_t[s, 128:256, 128:256] = q
        return carry

    lax.fori_loop(0, n_slot, set_diag, 0)

    def both(n):
        message_group(n - LAG)
        hidden_group(n)

    run(LAG, total_groups, both)
    run(total_groups - LAG, total_groups, message_group)

    def add_bias(s, carry):
        weight_sum = jnp.dot(
            cm[s].astype(BF16), diag[s, 0:128, 0:128], preferred_element_type=F32
        )
        msg[s] = msg[s] + weight_sum * b2_ref[...]
        return carry

    lax.fori_loop(0, n_slot, add_bias, 0)

    def gather_tile(tile, carry):
        total = None
        for s in range(n_slot):
            t, _ = tiles_of(s)
            term = msg[s] * jnp.where(t == tile, 1.0, 0.0)
            total = term if total is None else total + term
        part[tile] = total.astype(BF16)
        return carry

    lax.fori_loop(0, n_col, gather_tile, 0)
    msg_in[my_col] = part[my_col]

    def msg_copy(k, tile, src_index):
        return to_col(part.at[tile], msg_in.at[src_index], ms.at[k], mr.at[src_index], col_peer(k))

    each(n_col, lambda k: msg_copy(k, col_peer(k), my_col).start())

    def derivative_group(n):
        s, base = n // groups, lax.rem(n, groups) * PAIRS
        for b in range(PAIRS):
            ip = base + b
            slope = jnp.dot(
                w1d[...], slope_in[s, ip], preferred_element_type=F32
            ).astype(BF16)
            level = hid[s, ip]
            sig = jnp.asarray(1.0, BF16) - jnp.exp2(jnp.asarray(-1.0, BF16) - level)
            hid[s, ip] = slope * sig + level * row16(pair_row(ratio, s, ip))

    run(0, SPLIT, derivative_group)

    each(n_col, lambda k: msg_copy(k, col_peer(k), col_peer(k)).wait_recv())
    total = msg_in[0].astype(F32)
    for k in range(1, n_col):
        total = total + msg_in[k].astype(F32)
    pre = jnp.dot(total.astype(BF16), wo1_ref[...], preferred_element_type=F32) + bo1_ref[...]
    small = jnp.exp(-jnp.abs(pre))
    activated = (jnp.maximum(pre, 0.0) + jnp.log(1.0 + small) - LN2).astype(BF16)
    sig = jnp.where(pre >= 0.0, 1.0, small) / (1.0 + small)
    direction = lax.dot_general(
        jnp.broadcast_to(rw_ref[...], (8, 128)), wo2_ref[...].astype(F32),
        (((1,), (1,)), ((), ())), precision=lax.Precision.HIGHEST,
        preferred_element_type=F32,
    )[0:1, :]
    grad_own[...] = lax.dot_general(
        sig * direction, wo1_ref[...].astype(F32), (((1,), (1,)), ((), ())),
        precision=lax.Precision.HIGHEST, preferred_element_type=F32,
    ).astype(BF16)
    grad_all[my_col] = grad_own[...]

    def grad_copy(k, src_index):
        return to_col(grad_own, grad_all.at[src_index], gs.at[k], gr.at[src_index], col_peer(k))

    each(n_col, lambda k: grad_copy(k, my_col).start())
    update = jnp.dot(activated, wo2_ref[...], preferred_element_type=F32) + bo2_ref[...]
    fout_ref[...] = (feat_ref[...].astype(F32) + jnp.transpose(update)).astype(BF16)
    run(SPLIT, total_groups, derivative_group)
    each(n_col, lambda k: grad_copy(k, col_peer(k)).wait_recv())

    def spread_grad(s, carry):
        t, _ = tiles_of(s)
        grad_f[s] = grad_all[t].astype(F32)
        return carry

    lax.fori_loop(0, n_slot, spread_grad, 0)

    def dist_group(n):
        s, base = n // groups, lax.rem(n, groups) * PAIRS
        w2 = w2_ref[...]
        lhs = jnp.concatenate(
            [
                jnp.concatenate(
                    [
                        w2 * row16(grad_f[s, pl.ds(base + b, 1), :]),
                        w2 * row16(grad_f[s, pl.ds(base + b + half, 1), :]),
                    ],
                    axis=1,
                )
                for b in range(PAIRS)
            ],
            axis=0,
        )
        q = jnp.dot(lhs, diag_t[s], preferred_element_type=F32)
        for b in range(PAIRS):
            product = q[b * 128:(b + 1) * 128].astype(BF16) * hid[s, base + b]
            folded = (product[0:64] + product[64:128]).astype(F32)
            row = jnp.sum(folded, axis=0, keepdims=True)
            dgrad[s, pl.ds(base + b, 1), :] = row[:, 0:128]
            dgrad[s, pl.ds(base + b + half, 1), :] = row[:, 128:256]

    run(0, total_groups, dist_group)

    def force_slot(s, carry):
        g_b2 = (grad_f[s] * b2_ref[...]).astype(BF16)
        plain = jnp.dot(g_b2, diag_t[s, 0:128, 0:128], preferred_element_type=F32)
        d = dgrad[s] * (cm[s] * SLOPE) + cpm[s] * plain
        rows, cols = [], []
        for a in range(3):
            push = unit[s, a] * d
            cols.append(jnp.sum(push, axis=0, keepdims=True))
            rows.append(-jnp.sum(jnp.transpose(push), axis=0, keepdims=True))
        pad = [jnp.zeros((5, 128), F32)]
        rforce[s] = jnp.concatenate(rows + pad, axis=0)
        cforce[s] = jnp.concatenate(cols + pad, axis=0)
        return carry

    lax.fori_loop(0, n_slot, force_slot, 0)

    def spread(source, target, which, n):
        def one(tile, carry):
            total = None
            for s in range(n_slot):
                term = source[s] * jnp.where(tiles_of(s)[which] == tile, 1.0, 0.0)
                total = term if total is None else total + term
            target[tile] = total
            return carry
        lax.fori_loop(0, n, one, 0)

    spread(cforce, cpart, 1, n_row)
    spread(rforce, rpart, 0, n_col)
    cforce_in[my_row] = cpart[my_row]
    rforce_in[my_col] = rpart[my_col]

    def cforce_copy(k, tile, src_index):
        return to_row(cpart.at[tile], cforce_in.at[src_index], cfs.at[k], cfr.at[src_index], row_peer(k))

    def rforce_copy(k, tile, src_index):
        return to_col(rpart.at[tile], rforce_in.at[src_index], rfs.at[k], rfr.at[src_index], col_peer(k))

    each(n_row, lambda k: cforce_copy(k, row_peer(k), my_row).start())
    each(n_col, lambda k: rforce_copy(k, col_peer(k), my_col).start())

    each(n_row, lambda k: pos_col_copy(k, my_row).wait_send())
    each(n_col, lambda k: pos_row_copy(k, my_col).wait_send())
    each(n_chip, lambda k: proj_copy(k, my_row).wait_send())
    proj_hand(0).wait_send()
    each(n_chip, lambda k: proj_hand(k).wait_send())
    each(n_col, lambda k: msg_copy(k, col_peer(k), my_col).wait_send())
    each(n_col, lambda k: grad_copy(k, my_col).wait_send())

    each(n_col, lambda k: rforce_copy(k, col_peer(k), col_peer(k)).wait_recv())
    each(n_row, lambda k: cforce_copy(k, row_peer(k), row_peer(k)).wait_recv())
    force = rforce_in[0]
    for k in range(1, n_col):
        force = force + rforce_in[k]
    for k in range(n_row):
        force = force + cforce_in[k]
    force_ref[...] = force[0:3, :]
    each(n_row, lambda k: cforce_copy(k, row_peer(k), my_row).wait_send())
    each(n_col, lambda k: rforce_copy(k, col_peer(k), my_col).wait_send())


def solution(mesh):
    n_row, n_col = mesh.shape["row"], mesh.shape["col"]

    def local(features, positions, tile_pairs, pair_count, masks, w_in, w_f1, b_f1, w_f2, b_f2,
              w_o1, b_o1, w_o2, b_o2, read_w):
        n_slot = masks.shape[2]
        vmem = pl.BlockSpec(memory_space=pltpu.VMEM)
        smem = pl.BlockSpec(memory_space=pltpu.SMEM)
        tile = (128, 128)
        dma = pltpu.SemaphoreType.DMA
        return pl.pallas_call(
            functools.partial(kernel, n_row, n_col, n_slot),
            out_shape=(
                jax.ShapeDtypeStruct(features.shape, BF16),
                jax.ShapeDtypeStruct(positions.shape, F32),
            ),
            in_specs=[smem, smem] + [vmem] * 13,
            out_specs=(vmem, vmem),
            scratch_shapes=[
                pltpu.VMEM((n_col, 3, 128), F32),
                pltpu.VMEM((n_row, 3, 128), F32),
                pltpu.VMEM((n_row,) + tile, BF16),
                pltpu.VMEM(tile, BF16),
                pltpu.VMEM((128, 64), BF16),
                pltpu.VMEM(tile, F32),
                pltpu.VMEM((n_slot, 256, 256), BF16),
                pltpu.VMEM((n_slot, 256, 256), BF16),
                pltpu.VMEM((n_slot,) + tile, F32),
                pltpu.VMEM((n_slot,) + tile, F32),
                pltpu.VMEM((n_slot,) + tile, F32),
                pltpu.VMEM((n_slot,) + tile, F32),
                pltpu.VMEM((n_slot, 3) + tile, F32),
                pltpu.VMEM((n_slot, 64, 128, 256), BF16),
                pltpu.VMEM((n_slot, 64, 64, 256), BF16),
                pltpu.VMEM((n_slot,) + tile, F32),
                pltpu.VMEM((n_col,) + tile, BF16),
                pltpu.VMEM((n_col,) + tile, BF16),
                pltpu.VMEM(tile, BF16),
                pltpu.VMEM((n_col,) + tile, BF16),
                pltpu.VMEM((n_slot,) + tile, F32),
                pltpu.VMEM((n_slot,) + tile, F32),
                pltpu.VMEM((n_slot, 8, 128), F32),
                pltpu.VMEM((n_slot, 8, 128), F32),
                pltpu.VMEM((n_col, 8, 128), F32),
                pltpu.VMEM((n_row, 8, 128), F32),
                pltpu.VMEM((n_col, 8, 128), F32),
                pltpu.VMEM((n_row, 8, 128), F32),
                dma((n_row,)), dma((n_row,)),
                dma((n_col,)), dma((n_col,)),
                dma((n_row // 2,)), dma((n_row // 2,)), dma((n_row,)),
                dma((n_col,)), dma((n_col,)),
                dma((n_col,)), dma((n_col,)),
                dma((n_col,)), dma((n_col,)),
                dma((n_row,)), dma((n_row,)),
            ],
            compiler_params=pltpu.CompilerParams(
                collective_id=0, has_side_effects=True, vmem_limit_bytes=56 << 20
            ),
        )(
            tile_pairs.reshape(tile_pairs.shape[2:]), pair_count, features, positions,
            masks.reshape(masks.shape[2:]),
            w_in, w_f1, b_f1.reshape(1, -1), w_f2, b_f2.reshape(1, -1),
            w_o1, b_o1.reshape(1, -1), w_o2, b_o2.reshape(1, -1), read_w.reshape(1, -1),
        )

    split = P(None, ("row", "col"))
    return jax.shard_map(
        local, mesh=mesh,
        in_specs=(split, split, P("row", "col", None, None), P("row", "col"),
                  P("row", "col", None, None, None)) + (P(),) * 10,
        out_specs=(split, split), check_vma=False,
    )
```

```python
import functools
import math

import jax
import jax.numpy as jnp
from jax import lax
from jax.experimental import pallas as pl
from jax.experimental.pallas import tpu as pltpu
from jax.sharding import PartitionSpec as P

SOFTENING = 0.25
GAMMA_RBF = 10.0
CENTER_MAX = 10.0
CUTOFF = 12.0
LN2 = math.log(2.0)
SCALE = math.sqrt(GAMMA_RBF / LN2)
SLOPE = -2.0 * GAMMA_RBF / SCALE
F32 = jnp.float32
BF16 = jnp.bfloat16
MESH = pl.DeviceIdType.MESH
PAIRS = 32
HAND = 4
LAG = 5
SPLIT = 4


def cos_sin(x):
    y = x * x
    cos_acc = jnp.full_like(y, 1.0 / math.factorial(14)) * -1.0
    for n in (12, 10, 8, 6, 4, 2, 0):
        sign = 1.0 if (n // 2) % 2 == 0 else -1.0
        cos_acc = cos_acc * y + sign / math.factorial(n)
    sin_acc = jnp.full_like(y, 1.0 / math.factorial(13))
    for n in (11, 9, 7, 5, 3, 1):
        sign = 1.0 if ((n - 1) // 2) % 2 == 0 else -1.0
        sin_acc = sin_acc * y + sign / math.factorial(n)
    return cos_acc, sin_acc * x


def pieces(value):
    high = value.astype(BF16)
    rest = value - high.astype(F32)
    mid = rest.astype(BF16)
    low = (rest - mid.astype(F32)).astype(BF16)
    return high, mid, low


def row16(row):
    block = jnp.broadcast_to(row, (16, row.shape[1])).astype(BF16)
    return jnp.concatenate([block] * 8, axis=0)


def kernel(
    n_row, n_col, n_slot,
    pairs_ref, count_ref, feat_ref, pos_ref, mask_ref,
    w_in_ref, w1_ref, b1_ref, w2_ref, b2_ref, wo1_ref, bo1_ref, wo2_ref, bo2_ref, rw_ref,
    fout_ref, force_ref,
    pos_row, pos_col, proj_all,
    w1a, w1d, w2f, diag, diag_t,
    dist, cm, cpm, ratio, unit,
    hid, slope_in, msg, part, msg_in, grad_own, grad_all, grad_f, dgrad,
    rforce, cforce, rpart, cpart, rforce_in, cforce_in,
    prs, prr, pcs, pcr, js, jh, jr, ms, mr, gs, gr, rfs, rfr, cfs, cfr,
):
    my_row = lax.axis_index("row")
    my_col = lax.axis_index("col")
    half = 64

    def row_peer(k):
        return lax.rem(my_row + k, n_row)

    def col_peer(k):
        return lax.rem(my_col + k, n_col)

    def to_row(src, dst, ssem, rsem, peer):
        return pltpu.make_async_remote_copy(
            src_ref=src, dst_ref=dst, send_sem=ssem, recv_sem=rsem,
            device_id={"row": peer}, device_id_type=MESH,
        )

    def to_col(src, dst, ssem, rsem, peer):
        return pltpu.make_async_remote_copy(
            src_ref=src, dst_ref=dst, send_sem=ssem, recv_sem=rsem,
            device_id={"col": peer}, device_id_type=MESH,
        )

    def each(n, body):
        def step(k, carry):
            body(k)
            return carry
        lax.fori_loop(1, n, step, 0)

    barrier = pltpu.get_barrier_semaphore()
    each(n_row, lambda k: pl.semaphore_signal(
        barrier, inc=1, device_id={"row": row_peer(k)}, device_id_type=MESH))
    each(n_col, lambda k: pl.semaphore_signal(
        barrier, inc=1, device_id={"col": col_peer(k)}, device_id_type=MESH))

    def pos_row_copy(k, src_index):
        return to_col(pos_ref, pos_row.at[src_index], pcs.at[k], pcr.at[src_index], col_peer(k))

    def pos_col_copy(k, src_index):
        return to_row(pos_ref, pos_col.at[src_index], prs.at[k], prr.at[src_index], row_peer(k))

    core = lax.rem(my_row, 2)
    n_chip = n_row // 2

    def chip_peer(k):
        return lax.rem(my_row // 2 + k, n_chip) * 2 + core

    def proj_copy(k, src_index):
        return to_row(
            proj_all.at[my_row], proj_all.at[src_index], js.at[k], jr.at[src_index], chip_peer(k)
        )

    def proj_hand(k):
        return to_row(
            proj_all.at[chip_peer(k)], proj_all.at[chip_peer(k)], jh.at[k], jr.at[chip_peer(k)],
            my_row + 1 - 2 * core,
        )

    def proj_arrival(k):
        src = chip_peer(k) + 1 - 2 * core
        return to_row(
            proj_all.at[src], proj_all.at[src], jh.at[k], jr.at[src], my_row + 1 - 2 * core
        )

    pl.semaphore_wait(barrier, n_row - 1 + n_col - 1)
    each(n_row, lambda k: pos_col_copy(k, my_row).start())
    each(n_col, lambda k: pos_row_copy(k, my_col).start())

    feat_t = jnp.transpose(feat_ref[...].astype(F32))
    proj_all[my_row] = jnp.dot(
        feat_t.astype(BF16), w_in_ref[...], preferred_element_type=F32
    ).astype(BF16)
    each(n_chip, lambda k: proj_copy(k, my_row).start())
    proj_hand(0).start()
    pos_row[my_col] = pos_ref[...]
    pos_col[my_row] = pos_ref[...]

    bias = jnp.transpose(jnp.broadcast_to(b1_ref[...] - LN2, (128, 128)))
    high, mid, low = pieces(bias)
    lane = lax.broadcasted_iota(jnp.int32, (128, 128), 1)
    zero = jnp.zeros((128, 128), F32)
    extra = jnp.where(lane == 64, high.astype(F32), zero)
    extra = jnp.where(lane == 65, mid.astype(F32), extra)
    extra = jnp.where(lane == 66, low.astype(F32), extra)
    w1t = jnp.transpose(
        jnp.concatenate([w1_ref[...].astype(F32), jnp.zeros((64, 128), F32)], axis=0)
    )
    w1a[...] = (w1t + extra).astype(BF16)
    w1d[...] = w1t[:, 0:64].astype(BF16)
    w2f[...] = w2_ref[...].astype(F32)

    each(n_row, lambda k: pos_col_copy(k, row_peer(k)).wait_recv())
    each(n_col, lambda k: pos_row_copy(k, col_peer(k)).wait_recv())

    def tiles_of(s):
        t = jnp.clip(pairs_ref[0, s], 0, n_col - 1)
        c = jnp.clip(pairs_ref[1, s], 0, n_row - 1)
        return t, c

    def geometry(s, carry):
        t, c = tiles_of(s)
        pr = pos_row[t]
        pc = pos_col[c]
        seps = []
        d2 = None
        for a in range(3):
            column = jnp.transpose(jnp.broadcast_to(pr[a:a + 1, :], (128, 128)))
            sep = column - pc[a:a + 1, :]
            seps.append(sep)
            d2 = sep * sep if d2 is None else d2 + sep * sep
        d2 = d2 + SOFTENING
        d = jnp.sqrt(d2)
        inv = 1.0 / d
        cos_h, sin_h = cos_sin(d * (0.5 * math.pi / CUTOFF))
        listed = jnp.where(s < count_ref[0, 0], 1.0, 0.0)
        m = mask_ref[s].astype(F32) * listed
        dist[s] = d * SCALE
        cm[s] = m * (cos_h * cos_h)
        slope_c = (-math.pi / CUTOFF) * sin_h
        cpm[s] = m * (slope_c * cos_h)
        ratio[s] = (LN2 / SLOPE) * (slope_c / cos_h)
        for a in range(3):
            unit[s, a] = seps[a] * inv
        return carry

    lax.fori_loop(0, n_slot, geometry, 0)

    mu = lax.broadcasted_iota(jnp.int32, (64, 128), 0).astype(F32) * (
        CENTER_MAX / 63.0 * SCALE
    )
    ones = jnp.ones((16, 256), BF16)
    groups = half // PAIRS

    def pair_row(ref, s, ip):
        return jnp.concatenate(
            [ref[s, pl.ds(ip, 1), :], ref[s, pl.ds(ip + half, 1), :]], axis=1
        )

    def hidden_group(n):
        s, base = n // groups, lax.rem(n, groups) * PAIRS
        for b in range(PAIRS):
            ip = base + b
            x = jnp.concatenate(
                [dist[s, pl.ds(ip, 1), :] - mu, dist[s, pl.ds(ip + half, 1), :] - mu], axis=1
            )
            wide = jnp.exp2(-(x * x))
            slope_in[s, ip] = (wide * x).astype(BF16)
            g = wide.astype(BF16)
            pre = jnp.dot(
                w1a[:, 0:80], jnp.concatenate([g, ones], axis=0), preferred_element_type=F32
            ).astype(BF16)
            e = jnp.exp2(pre * jnp.asarray(1.0 / LN2, BF16))
            hid[s, ip] = lax.log2(e + jnp.asarray(0.5, BF16))

    def message_group(n):
        s, base = n // groups, lax.rem(n, groups) * PAIRS
        scaled = jnp.concatenate(
            [hid[s, base + b] * row16(pair_row(cm, s, base + b) * LN2) for b in range(PAIRS)],
            axis=0,
        )
        a = jnp.dot(scaled, diag[s], preferred_element_type=F32)
        w2 = w2f[...]
        for b in range(PAIRS):
            part_a = a[b * 128:(b + 1) * 128]
            msg[s, pl.ds(base + b, 1), :] = jnp.sum(part_a[:, 0:128] * w2, axis=0, keepdims=True)
            msg[s, pl.ds(base + b + half, 1), :] = jnp.sum(
                part_a[:, 128:256] * w2, axis=0, keepdims=True
            )

    total_groups = n_slot * groups

    def run(first, last, body):
        def step(n, carry):
            body(n)
            return carry
        lax.fori_loop(first, last, step, 0)

    run(0, HAND, hidden_group)

    def hand_on(k):
        proj_copy(k, chip_peer(k)).wait_recv()
        proj_hand(k).start()

    each(n_chip, hand_on)

    run(HAND, LAG, hidden_group)
    proj_arrival(0).wait_recv()
    each(n_chip, lambda k: proj_arrival(k).wait_recv())

    def set_diag(s, carry):
        _, c = tiles_of(s)
        p = proj_all[c]
        z = jnp.zeros((128, 128), BF16)
        diag[s, 0:128, 0:128] = p
        diag[s, 0:128, 128:256] = z
        diag[s, 128:256, 0:128] = z
        diag[s, 128:256, 128:256] = p
        q = jnp.transpose(p.astype(F32)).astype(BF16)
        diag_t[s, 0:128, 0:128] = q
        diag_t[s, 0:128, 128:256] = z
        diag_t[s, 128:256, 0:128] = z
        diag_t[s, 128:256, 128:256] = q
        return carry

    lax.fori_loop(0, n_slot, set_diag, 0)

    def both(n):
        message_group(n - LAG)
        hidden_group(n)

    run(LAG, total_groups, both)
    run(total_groups - LAG, total_groups, message_group)

    def add_bias(s, carry):
        weight_sum = jnp.dot(
            cm[s].astype(BF16), diag[s, 0:128, 0:128], preferred_element_type=F32
        )
        msg[s] = msg[s] + weight_sum * b2_ref[...]
        return carry

    lax.fori_loop(0, n_slot, add_bias, 0)

    def gather_tile(tile, carry):
        total = None
        for s in range(n_slot):
            t, _ = tiles_of(s)
            term = msg[s] * jnp.where(t == tile, 1.0, 0.0)
            total = term if total is None else total + term
        part[tile] = total.astype(BF16)
        return carry

    lax.fori_loop(0, n_col, gather_tile, 0)
    msg_in[my_col] = part[my_col]

    def msg_copy(k, tile, src_index):
        return to_col(part.at[tile], msg_in.at[src_index], ms.at[k], mr.at[src_index], col_peer(k))

    each(n_col, lambda k: msg_copy(k, col_peer(k), my_col).start())

    def derivative_group(n):
        s, base = n // groups, lax.rem(n, groups) * PAIRS
        for b in range(PAIRS):
            ip = base + b
            slope = jnp.dot(
                w1d[...], slope_in[s, ip], preferred_element_type=F32
            ).astype(BF16)
            level = hid[s, ip]
            sig = jnp.asarray(1.0, BF16) - jnp.exp2(jnp.asarray(-1.0, BF16) - level)
            hid[s, ip] = slope * sig + level * row16(pair_row(ratio, s, ip))

    run(0, SPLIT, derivative_group)

    each(n_col, lambda k: msg_copy(k, col_peer(k), col_peer(k)).wait_recv())
    total = msg_in[0].astype(F32)
    for k in range(1, n_col):
        total = total + msg_in[k].astype(F32)
    pre = jnp.dot(total.astype(BF16), wo1_ref[...], preferred_element_type=F32) + bo1_ref[...]
    small = jnp.exp(-jnp.abs(pre))
    activated = (jnp.maximum(pre, 0.0) + jnp.log(1.0 + small) - LN2).astype(BF16)
    sig = jnp.where(pre >= 0.0, 1.0, small) / (1.0 + small)
    direction = lax.dot_general(
        jnp.broadcast_to(rw_ref[...], (8, 128)), wo2_ref[...].astype(F32),
        (((1,), (1,)), ((), ())), precision=lax.Precision.HIGHEST,
        preferred_element_type=F32,
    )[0:1, :]
    grad_own[...] = lax.dot_general(
        sig * direction, wo1_ref[...].astype(F32), (((1,), (1,)), ((), ())),
        precision=lax.Precision.HIGHEST, preferred_element_type=F32,
    ).astype(BF16)
    grad_all[my_col] = grad_own[...]

    def grad_copy(k, src_index):
        return to_col(grad_own, grad_all.at[src_index], gs.at[k], gr.at[src_index], col_peer(k))

    each(n_col, lambda k: grad_copy(k, my_col).start())
    update = jnp.dot(activated, wo2_ref[...], preferred_element_type=F32) + bo2_ref[...]
    fout_ref[...] = (feat_ref[...].astype(F32) + jnp.transpose(update)).astype(BF16)
    run(SPLIT, total_groups, derivative_group)
    each(n_col, lambda k: grad_copy(k, col_peer(k)).wait_recv())

    def spread_grad(s, carry):
        t, _ = tiles_of(s)
        grad_f[s] = grad_all[t].astype(F32)
        return carry

    lax.fori_loop(0, n_slot, spread_grad, 0)

    def dist_group(n):
        s, base = n // groups, lax.rem(n, groups) * PAIRS
        w2 = w2_ref[...]
        lhs = jnp.concatenate(
            [
                jnp.concatenate(
                    [
                        w2 * row16(grad_f[s, pl.ds(base + b, 1), :]),
                        w2 * row16(grad_f[s, pl.ds(base + b + half, 1), :]),
                    ],
                    axis=1,
                )
                for b in range(PAIRS)
            ],
            axis=0,
        )
        q = jnp.dot(lhs, diag_t[s], preferred_element_type=F32)
        for b in range(PAIRS):
            product = q[b * 128:(b + 1) * 128].astype(BF16) * hid[s, base + b]
            folded = (product[0:64] + product[64:128]).astype(F32)
            row = jnp.sum(folded, axis=0, keepdims=True)
            dgrad[s, pl.ds(base + b, 1), :] = row[:, 0:128]
            dgrad[s, pl.ds(base + b + half, 1), :] = row[:, 128:256]

    run(0, total_groups, dist_group)

    def force_slot(s, carry):
        g_b2 = (grad_f[s] * b2_ref[...]).astype(BF16)
        plain = jnp.dot(g_b2, diag_t[s, 0:128, 0:128], preferred_element_type=F32)
        d = dgrad[s] * (cm[s] * SLOPE) + cpm[s] * plain
        rows, cols = [], []
        for a in range(3):
            push = unit[s, a] * d
            cols.append(jnp.sum(push, axis=0, keepdims=True))
            rows.append(-jnp.sum(jnp.transpose(push), axis=0, keepdims=True))
        pad = [jnp.zeros((5, 128), F32)]
        rforce[s] = jnp.concatenate(rows + pad, axis=0)
        cforce[s] = jnp.concatenate(cols + pad, axis=0)
        return carry

    lax.fori_loop(0, n_slot, force_slot, 0)

    def spread(source, target, which, n):
        def one(tile, carry):
            total = None
            for s in range(n_slot):
                term = source[s] * jnp.where(tiles_of(s)[which] == tile, 1.0, 0.0)
                total = term if total is None else total + term
            target[tile] = total[0:3]
            return carry
        lax.fori_loop(0, n, one, 0)

    spread(cforce, cpart, 1, n_row)
    spread(rforce, rpart, 0, n_col)
    cforce_in[my_row] = cpart[my_row]
    rforce_in[my_col] = rpart[my_col]

    def cforce_copy(k, tile, src_index):
        return to_row(cpart.at[tile], cforce_in.at[src_index], cfs.at[k], cfr.at[src_index], row_peer(k))

    def rforce_copy(k, tile, src_index):
        return to_col(rpart.at[tile], rforce_in.at[src_index], rfs.at[k], rfr.at[src_index], col_peer(k))

    each(n_row, lambda k: cforce_copy(k, row_peer(k), my_row).start())
    each(n_col, lambda k: rforce_copy(k, col_peer(k), my_col).start())

    each(n_row, lambda k: pos_col_copy(k, my_row).wait_send())
    each(n_col, lambda k: pos_row_copy(k, my_col).wait_send())
    each(n_chip, lambda k: proj_copy(k, my_row).wait_send())
    proj_hand(0).wait_send()
    each(n_chip, lambda k: proj_hand(k).wait_send())
    each(n_col, lambda k: msg_copy(k, col_peer(k), my_col).wait_send())
    each(n_col, lambda k: grad_copy(k, my_col).wait_send())

    each(n_col, lambda k: rforce_copy(k, col_peer(k), col_peer(k)).wait_recv())
    each(n_row, lambda k: cforce_copy(k, row_peer(k), row_peer(k)).wait_recv())
    force = rforce_in[0]
    for k in range(1, n_col):
        force = force + rforce_in[k]
    for k in range(n_row):
        force = force + cforce_in[k]
    force_ref[...] = force
    each(n_row, lambda k: cforce_copy(k, row_peer(k), my_row).wait_send())
    each(n_col, lambda k: rforce_copy(k, col_peer(k), my_col).wait_send())


def solution(mesh):
    n_row, n_col = mesh.shape["row"], mesh.shape["col"]

    def local(features, positions, tile_pairs, pair_count, masks, w_in, w_f1, b_f1, w_f2, b_f2,
              w_o1, b_o1, w_o2, b_o2, read_w):
        n_slot = masks.shape[2]
        vmem = pl.BlockSpec(memory_space=pltpu.VMEM)
        smem = pl.BlockSpec(memory_space=pltpu.SMEM)
        tile = (128, 128)
        dma = pltpu.SemaphoreType.DMA
        return pl.pallas_call(
            functools.partial(kernel, n_row, n_col, n_slot),
            out_shape=(
                jax.ShapeDtypeStruct(features.shape, BF16),
                jax.ShapeDtypeStruct(positions.shape, F32),
            ),
            in_specs=[smem, smem] + [vmem] * 13,
            out_specs=(vmem, vmem),
            scratch_shapes=[
                pltpu.VMEM((n_col, 3, 128), F32),
                pltpu.VMEM((n_row, 3, 128), F32),
                pltpu.VMEM((n_row,) + tile, BF16),
                pltpu.VMEM(tile, BF16),
                pltpu.VMEM((128, 64), BF16),
                pltpu.VMEM(tile, F32),
                pltpu.VMEM((n_slot, 256, 256), BF16),
                pltpu.VMEM((n_slot, 256, 256), BF16),
                pltpu.VMEM((n_slot,) + tile, F32),
                pltpu.VMEM((n_slot,) + tile, F32),
                pltpu.VMEM((n_slot,) + tile, F32),
                pltpu.VMEM((n_slot,) + tile, F32),
                pltpu.VMEM((n_slot, 3) + tile, F32),
                pltpu.VMEM((n_slot, 64, 128, 256), BF16),
                pltpu.VMEM((n_slot, 64, 64, 256), BF16),
                pltpu.VMEM((n_slot,) + tile, F32),
                pltpu.VMEM((n_col,) + tile, BF16),
                pltpu.VMEM((n_col,) + tile, BF16),
                pltpu.VMEM(tile, BF16),
                pltpu.VMEM((n_col,) + tile, BF16),
                pltpu.VMEM((n_slot,) + tile, F32),
                pltpu.VMEM((n_slot,) + tile, F32),
                pltpu.VMEM((n_slot, 8, 128), F32),
                pltpu.VMEM((n_slot, 8, 128), F32),
                pltpu.VMEM((n_col, 3, 128), F32),
                pltpu.VMEM((n_row, 3, 128), F32),
                pltpu.VMEM((n_col, 3, 128), F32),
                pltpu.VMEM((n_row, 3, 128), F32),
                dma((n_row,)), dma((n_row,)),
                dma((n_col,)), dma((n_col,)),
                dma((n_row // 2,)), dma((n_row // 2,)), dma((n_row,)),
                dma((n_col,)), dma((n_col,)),
                dma((n_col,)), dma((n_col,)),
                dma((n_col,)), dma((n_col,)),
                dma((n_row,)), dma((n_row,)),
            ],
            compiler_params=pltpu.CompilerParams(
                collective_id=0, has_side_effects=True, vmem_limit_bytes=56 << 20
            ),
        )(
            tile_pairs.reshape(tile_pairs.shape[2:]), pair_count, features, positions,
            masks.reshape(masks.shape[2:]),
            w_in, w_f1, b_f1.reshape(1, -1), w_f2, b_f2.reshape(1, -1),
            w_o1, b_o1.reshape(1, -1), w_o2, b_o2.reshape(1, -1), read_w.reshape(1, -1),
        )

    split = P(None, ("row", "col"))
    return jax.shard_map(
        local, mesh=mesh,
        in_specs=(split, split, P("row", "col", None, None), P("row", "col"),
                  P("row", "col", None, None, None)) + (P(),) * 10,
        out_specs=(split, split), check_vma=False,
    )
```

```python
import functools
import math

import jax
import jax.numpy as jnp
from jax import lax
from jax.experimental import pallas as pl
from jax.experimental.pallas import tpu as pltpu
from jax.sharding import PartitionSpec as P

SOFTENING = 0.25
GAMMA_RBF = 10.0
CENTER_MAX = 10.0
CUTOFF = 12.0
LN2 = math.log(2.0)
SCALE = math.sqrt(GAMMA_RBF / LN2)
SLOPE = -2.0 * GAMMA_RBF / SCALE
F32 = jnp.float32
BF16 = jnp.bfloat16
MESH = pl.DeviceIdType.MESH
PAIRS = 32
PASS = 0
HAND = 4
LAG = 5
SPLITS = (2, 5)


def cos_sin(x):
    y = x * x
    cos_acc = jnp.full_like(y, 1.0 / math.factorial(14)) * -1.0
    for n in (12, 10, 8, 6, 4, 2, 0):
        sign = 1.0 if (n // 2) % 2 == 0 else -1.0
        cos_acc = cos_acc * y + sign / math.factorial(n)
    sin_acc = jnp.full_like(y, 1.0 / math.factorial(13))
    for n in (11, 9, 7, 5, 3, 1):
        sign = 1.0 if ((n - 1) // 2) % 2 == 0 else -1.0
        sin_acc = sin_acc * y + sign / math.factorial(n)
    return cos_acc, sin_acc * x


def pieces(value):
    high = value.astype(BF16)
    rest = value - high.astype(F32)
    mid = rest.astype(BF16)
    low = (rest - mid.astype(F32)).astype(BF16)
    return high, mid, low


def row16(row):
    block = jnp.broadcast_to(row, (16, row.shape[1])).astype(BF16)
    return jnp.concatenate([block] * 8, axis=0)


def kernel(
    n_row, n_col, n_slot,
    pairs_ref, count_ref, feat_ref, pos_ref, mask_ref,
    w_in_ref, w1_ref, b1_ref, w2_ref, b2_ref, wo1_ref, bo1_ref, wo2_ref, bo2_ref, rw_ref,
    fout_ref, force_ref,
    pos_row, pos_col, proj_all,
    w1a, w1d, w2f, diag, diag_t,
    dist, cm, cpm, ratio, unit,
    hid, slope_in, msg, part, msg_in, grad_own, grad_a, grad_b, update, grad_f, dgrad,
    rforce, cforce, rpart, cpart, rforce_in, cforce_in,
    prs, prr, pcs, pcr, js, jt, jh, jr, ms, mr, gs, gr, rfs, rfr, cfs, cfr,
):
    my_row = lax.axis_index("row")
    my_col = lax.axis_index("col")
    half = 64
    grad_all = (grad_a, grad_b)

    def row_peer(k):
        return lax.rem(my_row + k, n_row)

    def col_peer(k):
        return lax.rem(my_col + k, n_col)

    def to_row(src, dst, ssem, rsem, peer):
        return pltpu.make_async_remote_copy(
            src_ref=src, dst_ref=dst, send_sem=ssem, recv_sem=rsem,
            device_id={"row": peer}, device_id_type=MESH,
        )

    def to_col(src, dst, ssem, rsem, peer):
        return pltpu.make_async_remote_copy(
            src_ref=src, dst_ref=dst, send_sem=ssem, recv_sem=rsem,
            device_id={"col": peer}, device_id_type=MESH,
        )

    def each(n, body):
        def step(k, carry):
            body(k)
            return carry
        lax.fori_loop(1, n, step, 0)

    barrier = pltpu.get_barrier_semaphore()
    each(n_row, lambda k: pl.semaphore_signal(
        barrier, inc=1, device_id={"row": row_peer(k)}, device_id_type=MESH))
    each(n_col, lambda k: pl.semaphore_signal(
        barrier, inc=1, device_id={"col": col_peer(k)}, device_id_type=MESH))

    def pos_row_copy(k, src_index):
        return to_col(pos_ref, pos_row.at[src_index], pcs.at[k], pcr.at[src_index], col_peer(k))

    def pos_col_copy(k, src_index):
        return to_row(pos_ref, pos_col.at[src_index], prs.at[k], prr.at[src_index], row_peer(k))

    core = lax.rem(my_row, 2)
    n_ring = n_row // 4
    ring = my_row // (2 * n_ring)
    spot = lax.rem(my_row // 2, n_ring)

    def on_ring(which, k):
        return (which * n_ring + lax.rem(spot + k, n_ring)) * 2 + core

    def other_core(row):
        return row + 1 - 2 * core

    def near(k):
        return on_ring(ring, k)

    def far(k):
        return on_ring(1 - ring, k)

    def tile_copy(tile, sem, peer):
        return to_row(proj_all.at[tile], proj_all.at[tile], sem, jr.at[tile], peer)

    def ring_copy(k):
        return tile_copy(my_row, js.at[k], near(k))

    def twin_copy(k):
        return tile_copy(near(k), jt.at[k], far(0))

    def hand_near(k):
        return tile_copy(near(k), jh.at[k], other_core(my_row))

    def hand_far(k):
        return tile_copy(far(k), jh.at[n_ring + k], other_core(my_row))

    def arrival(tile):
        tile_copy(tile, js.at[0], other_core(my_row)).wait_recv()

    def every(n, body):
        body(0)
        each(n, body)

    pl.semaphore_wait(barrier, n_row - 1 + n_col - 1)
    each(n_row, lambda k: pos_col_copy(k, my_row).start())
    each(n_col, lambda k: pos_row_copy(k, my_col).start())

    feat_t = jnp.transpose(feat_ref[...].astype(F32))
    proj_all[my_row] = jnp.dot(
        feat_t.astype(BF16), w_in_ref[...], preferred_element_type=F32
    ).astype(BF16)
    each(n_ring, lambda k: ring_copy(k).start())
    twin_copy(0).start()
    hand_near(0).start()
    pos_row[my_col] = pos_ref[...]
    pos_col[my_row] = pos_ref[...]

    bias = jnp.transpose(jnp.broadcast_to(b1_ref[...] - LN2, (128, 128)))
    high, mid, low = pieces(bias)
    lane = lax.broadcasted_iota(jnp.int32, (128, 128), 1)
    zero = jnp.zeros((128, 128), F32)
    extra = jnp.where(lane == 64, high.astype(F32), zero)
    extra = jnp.where(lane == 65, mid.astype(F32), extra)
    extra = jnp.where(lane == 66, low.astype(F32), extra)
    w1t = jnp.transpose(
        jnp.concatenate([w1_ref[...].astype(F32), jnp.zeros((64, 128), F32)], axis=0)
    )
    w1a[...] = (w1t + extra).astype(BF16)
    w1d[...] = w1t[:, 0:64].astype(BF16)
    w2f[...] = w2_ref[...].astype(F32)

    each(n_row, lambda k: pos_col_copy(k, row_peer(k)).wait_recv())
    each(n_col, lambda k: pos_row_copy(k, col_peer(k)).wait_recv())

    def tiles_of(s):
        t = jnp.clip(pairs_ref[0, s], 0, n_col - 1)
        c = jnp.clip(pairs_ref[1, s], 0, n_row - 1)
        return t, c

    def geometry(s, carry):
        t, c = tiles_of(s)
        pr = pos_row[t]
        pc = pos_col[c]
        seps = []
        d2 = None
        for a in range(3):
            column = jnp.transpose(jnp.broadcast_to(pr[a:a + 1, :], (128, 128)))
            sep = column - pc[a:a + 1, :]
            seps.append(sep)
            d2 = sep * sep if d2 is None else d2 + sep * sep
        d2 = d2 + SOFTENING
        d = jnp.sqrt(d2)
        inv = 1.0 / d
        cos_h, sin_h = cos_sin(d * (0.5 * math.pi / CUTOFF))
        listed = jnp.where(s < count_ref[0, 0], 1.0, 0.0)
        m = mask_ref[s].astype(F32) * listed
        dist[s] = d * SCALE
        cm[s] = m * (cos_h * cos_h)
        slope_c = (-math.pi / CUTOFF) * sin_h
        cpm[s] = m * (slope_c * cos_h)
        ratio[s] = (LN2 / SLOPE) * (slope_c / cos_h)
        for a in range(3):
            unit[s, a] = seps[a] * inv
        return carry

    lax.fori_loop(0, n_slot, geometry, 0)

    mu = lax.broadcasted_iota(jnp.int32, (64, 128), 0).astype(F32) * (
        CENTER_MAX / 63.0 * SCALE
    )
    ones = jnp.ones((16, 256), BF16)
    groups = half // PAIRS

    def place(n):
        return lax.rem(n, n_slot), n // n_slot * PAIRS

    def pair_row(ref, s, row):
        return jnp.concatenate(
            [ref[s, pl.ds(row, 1), :], ref[s, pl.ds(row + PAIRS, 1), :]], axis=1
        )

    def hidden_group(n):
        s, base = place(n)
        for b in range(PAIRS):
            ip = base + b
            x = jnp.concatenate(
                [
                    dist[s, pl.ds(2 * base + b, 1), :] - mu,
                    dist[s, pl.ds(2 * base + b + PAIRS, 1), :] - mu,
                ],
                axis=1,
            )
            wide = jnp.exp2(-(x * x))
            slope_in[s, ip] = (wide * x).astype(BF16)
            g = wide.astype(BF16)
            pre = jnp.dot(
                w1a[:, 0:80], jnp.concatenate([g, ones], axis=0), preferred_element_type=F32
            ).astype(BF16)
            e = jnp.exp2(pre * jnp.asarray(1.0 / LN2, BF16))
            hid[s, ip] = lax.log2(e + jnp.asarray(0.5, BF16))

    def message_group(n):
        s, base = place(n)
        scaled = jnp.concatenate(
            [hid[s, base + b] * row16(pair_row(cm, s, 2 * base + b) * LN2) for b in range(PAIRS)],
            axis=0,
        )
        a = jnp.dot(scaled, diag[s], preferred_element_type=F32)
        w2 = w2f[...]
        for b in range(PAIRS):
            part_a = a[b * 128:(b + 1) * 128]
            msg[s, pl.ds(2 * base + b, 1), :] = jnp.sum(part_a[:, 0:128] * w2, axis=0, keepdims=True)
            msg[s, pl.ds(2 * base + b + PAIRS, 1), :] = jnp.sum(
                part_a[:, 128:256] * w2, axis=0, keepdims=True
            )

    total_groups = n_slot * groups

    def run(first, last, body):
        def step(n, carry):
            body(n)
            return carry
        lax.fori_loop(first, last, step, 0)

    def pass_near(k):
        arrival(near(k))
        twin_copy(k).start()
        hand_near(k).start()

    def pass_far(k):
        arrival(far(k))
        hand_far(k).start()

    def arrive_pair(k):
        arrival(other_core(near(k)))
        arrival(other_core(far(k)))

    run(0, PASS, hidden_group)
    each(n_ring, pass_near)
    run(PASS, HAND, hidden_group)
    every(n_ring, pass_far)
    run(HAND, LAG, hidden_group)
    every(n_ring, arrive_pair)

    def set_diag(s, carry):
        _, c = tiles_of(s)
        p = proj_all[c]
        z = jnp.zeros((128, 128), BF16)
        diag[s, 0:128, 0:128] = p
        diag[s, 0:128, 128:256] = z
        diag[s, 128:256, 0:128] = z
        diag[s, 128:256, 128:256] = p
        q = jnp.transpose(p.astype(F32)).astype(BF16)
        diag_t[s, 0:128, 0:128] = q
        diag_t[s, 0:128, 128:256] = z
        diag_t[s, 128:256, 0:128] = z
        diag_t[s, 128:256, 128:256] = q
        return carry

    lax.fori_loop(0, n_slot, set_diag, 0)

    def both(n):
        message_group(n - LAG)
        hidden_group(n)

    run(LAG, total_groups, both)

    span = 2 * PAIRS

    def part_rows(h):
        return slice(h * span, (h + 1) * span)

    def add_bias(h):
        def body(s, carry):
            weight_sum = jnp.dot(
                cm[s, part_rows(h)].astype(BF16), diag[s, 0:128, 0:128],
                preferred_element_type=F32,
            )
            msg[s, part_rows(h)] = msg[s, part_rows(h)] + weight_sum * b2_ref[...]
            return carry
        lax.fori_loop(0, n_slot, body, 0)

    def gather_part(h):
        def body(tile, carry):
            total = None
            for s in range(n_slot):
                t, _ = tiles_of(s)
                term = msg[s, part_rows(h)] * jnp.where(t == tile, 1.0, 0.0)
                total = term if total is None else total + term
            part[h, tile] = total.astype(BF16)
            return carry
        lax.fori_loop(0, n_col, body, 0)
        msg_in[h, my_col] = part[h, my_col]

    def msg_copy(h, k, tile, src_index):
        return to_col(
            part.at[h, tile], msg_in.at[h, src_index], ms.at[h * n_col + k],
            mr.at[h * n_col + src_index], col_peer(k),
        )

    for h in range(groups):
        run(max(total_groups - LAG, h * n_slot), (h + 1) * n_slot, message_group)
        add_bias(h)
        gather_part(h)
        each(n_col, lambda k, h=h: msg_copy(h, k, col_peer(k), my_col).start())

    def derivative_group(n):
        s, base = place(n)
        for b in range(PAIRS):
            ip = base + b
            slope = jnp.dot(
                w1d[...], slope_in[s, ip], preferred_element_type=F32
            ).astype(BF16)
            level = hid[s, ip]
            sig = jnp.asarray(1.0, BF16) - jnp.exp2(jnp.asarray(-1.0, BF16) - level)
            hid[s, ip] = slope * sig + level * row16(pair_row(ratio, s, 2 * base + b))

    direction = lax.dot_general(
        jnp.broadcast_to(rw_ref[...], (8, 128)), wo2_ref[...].astype(F32),
        (((1,), (1,)), ((), ())), precision=lax.Precision.HIGHEST,
        preferred_element_type=F32,
    )[0:1, :]

    def grad_copy(h, k, src_index):
        return to_col(
            grad_own.at[h], grad_all[h].at[src_index], gs.at[h * n_col + k],
            gr.at[h * n_col + src_index], col_peer(k),
        )

    def atom_update(h):
        each(n_col, lambda k: msg_copy(h, k, col_peer(k), col_peer(k)).wait_recv())
        total = msg_in[h, 0].astype(F32)
        for k in range(1, n_col):
            total = total + msg_in[h, k].astype(F32)
        act_in = jnp.dot(total.astype(BF16), wo1_ref[...], preferred_element_type=F32) + bo1_ref[...]
        small = jnp.exp(-jnp.abs(act_in))
        activated = (jnp.maximum(act_in, 0.0) + jnp.log(1.0 + small) - LN2).astype(BF16)
        sig = jnp.where(act_in >= 0.0, 1.0, small) / (1.0 + small)
        grad_own[h] = lax.dot_general(
            sig * direction, wo1_ref[...].astype(F32), (((1,), (1,)), ((), ())),
            precision=lax.Precision.HIGHEST, preferred_element_type=F32,
        ).astype(BF16)
        grad_all[h][my_col] = grad_own[h]
        each(n_col, lambda k: grad_copy(h, k, my_col).start())
        update[part_rows(h)] = (
            jnp.dot(activated, wo2_ref[...], preferred_element_type=F32) + bo2_ref[...]
        )

    done = 0
    for h in range(groups):
        run(done, SPLITS[h], derivative_group)
        done = SPLITS[h]
        atom_update(h)
    run(done, total_groups, derivative_group)
    fout_ref[...] = (feat_ref[...].astype(F32) + jnp.transpose(update[...])).astype(BF16)

    def spread_grad(h):
        def body(s, carry):
            t, _ = tiles_of(s)
            grad_f[s, part_rows(h)] = grad_all[h][t].astype(F32)
            return carry
        lax.fori_loop(0, n_slot, body, 0)

    def dist_group(n):
        s, base = place(n)
        w2 = w2_ref[...]
        lhs = jnp.concatenate(
            [
                jnp.concatenate(
                    [
                        w2 * row16(grad_f[s, pl.ds(2 * base + b, 1), :]),
                        w2 * row16(grad_f[s, pl.ds(2 * base + b + PAIRS, 1), :]),
                    ],
                    axis=1,
                )
                for b in range(PAIRS)
            ],
            axis=0,
        )
        q = jnp.dot(lhs, diag_t[s], preferred_element_type=F32)
        for b in range(PAIRS):
            product = q[b * 128:(b + 1) * 128].astype(BF16) * hid[s, base + b]
            folded = (product[0:64] + product[64:128]).astype(F32)
            row = jnp.sum(folded, axis=0, keepdims=True)
            dgrad[s, pl.ds(2 * base + b, 1), :] = row[:, 0:128]
            dgrad[s, pl.ds(2 * base + b + PAIRS, 1), :] = row[:, 128:256]

    for h in range(groups):
        each(n_col, lambda k, h=h: grad_copy(h, k, col_peer(k)).wait_recv())
        spread_grad(h)
        run(h * n_slot, (h + 1) * n_slot, dist_group)

    def force_slot(s, carry):
        g_b2 = (grad_f[s] * b2_ref[...]).astype(BF16)
        plain = jnp.dot(g_b2, diag_t[s, 0:128, 0:128], preferred_element_type=F32)
        d = dgrad[s] * (cm[s] * SLOPE) + cpm[s] * plain
        rows, cols = [], []
        for a in range(3):
            push = unit[s, a] * d
            cols.append(jnp.sum(push, axis=0, keepdims=True))
            rows.append(-jnp.sum(jnp.transpose(push), axis=0, keepdims=True))
        pad = [jnp.zeros((5, 128), F32)]
        rforce[s] = jnp.concatenate(rows + pad, axis=0)
        cforce[s] = jnp.concatenate(cols + pad, axis=0)
        return carry

    lax.fori_loop(0, n_slot, force_slot, 0)

    def spread(source, target, which, n):
        def one(tile, carry):
            total = None
            for s in range(n_slot):
                term = source[s] * jnp.where(tiles_of(s)[which] == tile, 1.0, 0.0)
                total = term if total is None else total + term
            target[tile] = total[0:3]
            return carry
        lax.fori_loop(0, n, one, 0)

    spread(cforce, cpart, 1, n_row)
    spread(rforce, rpart, 0, n_col)
    cforce_in[my_row] = cpart[my_row]
    rforce_in[my_col] = rpart[my_col]

    def cforce_copy(k, tile, src_index):
        return to_row(cpart.at[tile], cforce_in.at[src_index], cfs.at[k], cfr.at[src_index], row_peer(k))

    def rforce_copy(k, tile, src_index):
        return to_col(rpart.at[tile], rforce_in.at[src_index], rfs.at[k], rfr.at[src_index], col_peer(k))

    each(n_row, lambda k: cforce_copy(k, row_peer(k), my_row).start())
    each(n_col, lambda k: rforce_copy(k, col_peer(k), my_col).start())

    each(n_row, lambda k: pos_col_copy(k, my_row).wait_send())
    each(n_col, lambda k: pos_row_copy(k, my_col).wait_send())
    each(n_ring, lambda k: ring_copy(k).wait_send())
    every(n_ring, lambda k: twin_copy(k).wait_send())
    every(n_ring, lambda k: hand_near(k).wait_send())
    every(n_ring, lambda k: hand_far(k).wait_send())
    for h in range(groups):
        each(n_col, lambda k, h=h: msg_copy(h, k, col_peer(k), my_col).wait_send())
        each(n_col, lambda k, h=h: grad_copy(h, k, my_col).wait_send())

    each(n_col, lambda k: rforce_copy(k, col_peer(k), col_peer(k)).wait_recv())
    each(n_row, lambda k: cforce_copy(k, row_peer(k), row_peer(k)).wait_recv())
    force = rforce_in[0]
    for k in range(1, n_col):
        force = force + rforce_in[k]
    for k in range(n_row):
        force = force + cforce_in[k]
    force_ref[...] = force
    each(n_row, lambda k: cforce_copy(k, row_peer(k), my_row).wait_send())
    each(n_col, lambda k: rforce_copy(k, col_peer(k), my_col).wait_send())


def solution(mesh):
    n_row, n_col = mesh.shape["row"], mesh.shape["col"]

    def local(features, positions, tile_pairs, pair_count, masks, w_in, w_f1, b_f1, w_f2, b_f2,
              w_o1, b_o1, w_o2, b_o2, read_w):
        n_slot = masks.shape[2]
        vmem = pl.BlockSpec(memory_space=pltpu.VMEM)
        smem = pl.BlockSpec(memory_space=pltpu.SMEM)
        tile = (128, 128)
        dma = pltpu.SemaphoreType.DMA
        return pl.pallas_call(
            functools.partial(kernel, n_row, n_col, n_slot),
            out_shape=(
                jax.ShapeDtypeStruct(features.shape, BF16),
                jax.ShapeDtypeStruct(positions.shape, F32),
            ),
            in_specs=[smem, smem] + [vmem] * 13,
            out_specs=(vmem, vmem),
            scratch_shapes=[
                pltpu.VMEM((n_col, 3, 128), F32),
                pltpu.VMEM((n_row, 3, 128), F32),
                pltpu.VMEM((n_row,) + tile, BF16),
                pltpu.VMEM(tile, BF16),
                pltpu.VMEM((128, 64), BF16),
                pltpu.VMEM(tile, F32),
                pltpu.VMEM((n_slot, 256, 256), BF16),
                pltpu.VMEM((n_slot, 256, 256), BF16),
                pltpu.VMEM((n_slot,) + tile, F32),
                pltpu.VMEM((n_slot,) + tile, F32),
                pltpu.VMEM((n_slot,) + tile, F32),
                pltpu.VMEM((n_slot,) + tile, F32),
                pltpu.VMEM((n_slot, 3) + tile, F32),
                pltpu.VMEM((n_slot, 64, 128, 256), BF16),
                pltpu.VMEM((n_slot, 64, 64, 256), BF16),
                pltpu.VMEM((n_slot,) + tile, F32),
                pltpu.VMEM((64 // PAIRS, n_col, 2 * PAIRS, 128), BF16),
                pltpu.VMEM((64 // PAIRS, n_col, 2 * PAIRS, 128), BF16),
                pltpu.VMEM((64 // PAIRS, 2 * PAIRS, 128), BF16),
                pltpu.VMEM((n_col, 2 * PAIRS, 128), BF16),
                pltpu.VMEM((n_col, 2 * PAIRS, 128), BF16),
                pltpu.VMEM(tile, F32),
                pltpu.VMEM((n_slot,) + tile, F32),
                pltpu.VMEM((n_slot,) + tile, F32),
                pltpu.VMEM((n_slot, 8, 128), F32),
                pltpu.VMEM((n_slot, 8, 128), F32),
                pltpu.VMEM((n_col, 3, 128), F32),
                pltpu.VMEM((n_row, 3, 128), F32),
                pltpu.VMEM((n_col, 3, 128), F32),
                pltpu.VMEM((n_row, 3, 128), F32),
                dma((n_row,)), dma((n_row,)),
                dma((n_col,)), dma((n_col,)),
                dma((n_row // 4,)), dma((n_row // 4,)), dma((n_row // 2,)), dma((n_row,)),
                dma((64 // PAIRS * n_col,)), dma((64 // PAIRS * n_col,)),
                dma((64 // PAIRS * n_col,)), dma((64 // PAIRS * n_col,)),
                dma((n_col,)), dma((n_col,)),
                dma((n_row,)), dma((n_row,)),
            ],
            compiler_params=pltpu.CompilerParams(
                collective_id=0, has_side_effects=True, vmem_limit_bytes=56 << 20
            ),
        )(
            tile_pairs.reshape(tile_pairs.shape[2:]), pair_count, features, positions,
            masks.reshape(masks.shape[2:]),
            w_in, w_f1, b_f1.reshape(1, -1), w_f2, b_f2.reshape(1, -1),
            w_o1, b_o1.reshape(1, -1), w_o2, b_o2.reshape(1, -1), read_w.reshape(1, -1),
        )

    split = P(None, ("row", "col"))
    return jax.shard_map(
        local, mesh=mesh,
        in_specs=(split, split, P("row", "col", None, None), P("row", "col"),
                  P("row", "col", None, None, None)) + (P(),) * 10,
        out_specs=(split, split), check_vma=False,
    )
```

```python
import functools
import math

import jax
import jax.numpy as jnp
from jax import lax
from jax.experimental import pallas as pl
from jax.experimental.pallas import tpu as pltpu
from jax.sharding import PartitionSpec as P

SOFTENING = 0.25
GAMMA_RBF = 10.0
CENTER_MAX = 10.0
CUTOFF = 12.0
LN2 = math.log(2.0)
SCALE = math.sqrt(GAMMA_RBF / LN2)
SLOPE = -2.0 * GAMMA_RBF / SCALE
F32 = jnp.float32
BF16 = jnp.bfloat16
MESH = pl.DeviceIdType.MESH
PAIRS = 32
PASS = 0
HAND = 5
LAG = 6
SPLITS = (2, 5)


def cos_sin(x):
    y = x * x
    cos_acc = jnp.full_like(y, 1.0 / math.factorial(14)) * -1.0
    for n in (12, 10, 8, 6, 4, 2, 0):
        sign = 1.0 if (n // 2) % 2 == 0 else -1.0
        cos_acc = cos_acc * y + sign / math.factorial(n)
    sin_acc = jnp.full_like(y, 1.0 / math.factorial(13))
    for n in (11, 9, 7, 5, 3, 1):
        sign = 1.0 if ((n - 1) // 2) % 2 == 0 else -1.0
        sin_acc = sin_acc * y + sign / math.factorial(n)
    return cos_acc, sin_acc * x


def pieces(value):
    high = value.astype(BF16)
    rest = value - high.astype(F32)
    mid = rest.astype(BF16)
    low = (rest - mid.astype(F32)).astype(BF16)
    return high, mid, low


def row16(row):
    block = jnp.broadcast_to(row, (16, row.shape[1])).astype(BF16)
    return jnp.concatenate([block] * 8, axis=0)


def kernel(
    n_row, n_col, n_slot,
    pairs_ref, count_ref, feat_ref, pos_ref, mask_ref,
    w_in_ref, w1_ref, b1_ref, w2_ref, b2_ref, wo1_ref, bo1_ref, wo2_ref, bo2_ref, rw_ref,
    fout_ref, force_ref,
    pos_row, pos_col, proj_all,
    w1a, w1d, w2f, diag, diag_t,
    dist, cm, cpm, ratio, unit,
    hid, slope_in, msg, part, msg_in, grad_own, grad_a, grad_b, update, grad_f, dgrad,
    rforce, cforce, rpart, cpart, rforce_in, cforce_in,
    prs, prr, pcs, pcr, js, jt, jh, jr, ms, mr, gs, gr, rfs, rfr, cfs, cfr,
):
    my_row = lax.axis_index("row")
    my_col = lax.axis_index("col")
    half = 64
    grad_all = (grad_a, grad_b)

    def row_peer(k):
        return lax.rem(my_row + k, n_row)

    def col_peer(k):
        return lax.rem(my_col + k, n_col)

    def to_row(src, dst, ssem, rsem, peer):
        return pltpu.make_async_remote_copy(
            src_ref=src, dst_ref=dst, send_sem=ssem, recv_sem=rsem,
            device_id={"row": peer}, device_id_type=MESH,
        )

    def to_col(src, dst, ssem, rsem, peer):
        return pltpu.make_async_remote_copy(
            src_ref=src, dst_ref=dst, send_sem=ssem, recv_sem=rsem,
            device_id={"col": peer}, device_id_type=MESH,
        )

    def each(n, body):
        def step(k, carry):
            body(k)
            return carry
        lax.fori_loop(1, n, step, 0)

    barrier = pltpu.get_barrier_semaphore()
    each(n_row, lambda k: pl.semaphore_signal(
        barrier, inc=1, device_id={"row": row_peer(k)}, device_id_type=MESH))
    each(n_col, lambda k: pl.semaphore_signal(
        barrier, inc=1, device_id={"col": col_peer(k)}, device_id_type=MESH))

    def pos_row_copy(k, src_index):
        return to_col(pos_ref, pos_row.at[src_index], pcs.at[k], pcr.at[src_index], col_peer(k))

    def pos_col_copy(k, src_index):
        return to_row(pos_ref, pos_col.at[src_index], prs.at[k], prr.at[src_index], row_peer(k))

    core = lax.rem(my_row, 2)
    n_ring = n_row // 4
    ring = my_row // (2 * n_ring)
    spot = lax.rem(my_row // 2, n_ring)

    def on_ring(which, k):
        return (which * n_ring + lax.rem(spot + k, n_ring)) * 2 + core

    def other_core(row):
        return row + 1 - 2 * core

    def near(k):
        return on_ring(ring, k)

    def far(k):
        return on_ring(1 - ring, k)

    def tile_copy(tile, sem, peer):
        return to_row(proj_all.at[tile], proj_all.at[tile], sem, jr.at[tile], peer)

    def ring_copy(k):
        return tile_copy(my_row, js.at[k], near(k))

    def twin_copy(k):
        return tile_copy(near(k), jt.at[k], far(0))

    def hand_near(k):
        return tile_copy(near(k), jh.at[k], other_core(my_row))

    def hand_far(k):
        return tile_copy(far(k), jh.at[n_ring + k], other_core(my_row))

    def arrival(tile):
        tile_copy(tile, js.at[0], other_core(my_row)).wait_recv()

    def every(n, body):
        body(0)
        each(n, body)

    pl.semaphore_wait(barrier, n_row - 1 + n_col - 1)
    each(n_row, lambda k: pos_col_copy(k, my_row).start())
    each(n_col, lambda k: pos_row_copy(k, my_col).start())

    feat_t = jnp.transpose(feat_ref[...].astype(F32))
    proj_all[my_row] = jnp.dot(
        feat_t.astype(BF16), w_in_ref[...], preferred_element_type=F32
    ).astype(BF16)
    each(n_ring, lambda k: ring_copy(k).start())
    twin_copy(0).start()
    hand_near(0).start()
    pos_row[my_col] = pos_ref[...]
    pos_col[my_row] = pos_ref[...]

    bias = jnp.transpose(jnp.broadcast_to(b1_ref[...] - LN2, (128, 128)))
    high, mid, low = pieces(bias)
    lane = lax.broadcasted_iota(jnp.int32, (128, 128), 1)
    zero = jnp.zeros((128, 128), F32)
    extra = jnp.where(lane == 64, high.astype(F32), zero)
    extra = jnp.where(lane == 65, mid.astype(F32), extra)
    extra = jnp.where(lane == 66, low.astype(F32), extra)
    w1t = jnp.transpose(
        jnp.concatenate([w1_ref[...].astype(F32), jnp.zeros((64, 128), F32)], axis=0)
    )
    w1a[...] = (w1t + extra).astype(BF16)
    w1d[...] = w1t[:, 0:64].astype(BF16)
    w2f[...] = w2_ref[...].astype(F32)

    each(n_row, lambda k: pos_col_copy(k, row_peer(k)).wait_recv())
    each(n_col, lambda k: pos_row_copy(k, col_peer(k)).wait_recv())

    def tiles_of(s):
        t = jnp.clip(pairs_ref[0, s], 0, n_col - 1)
        c = jnp.clip(pairs_ref[1, s], 0, n_row - 1)
        return t, c

    def geometry(s, carry):
        t, c = tiles_of(s)
        pr = pos_row[t]
        pc = pos_col[c]
        seps = []
        d2 = None
        for a in range(3):
            column = jnp.transpose(jnp.broadcast_to(pr[a:a + 1, :], (128, 128)))
            sep = column - pc[a:a + 1, :]
            seps.append(sep)
            d2 = sep * sep if d2 is None else d2 + sep * sep
        d2 = d2 + SOFTENING
        d = jnp.sqrt(d2)
        inv = 1.0 / d
        cos_h, sin_h = cos_sin(d * (0.5 * math.pi / CUTOFF))
        listed = jnp.where(s < count_ref[0, 0], 1.0, 0.0)
        m = mask_ref[s].astype(F32) * listed
        dist[s] = d * SCALE
        cm[s] = m * (cos_h * cos_h)
        slope_c = (-math.pi / CUTOFF) * sin_h
        cpm[s] = m * (slope_c * cos_h)
        ratio[s] = (LN2 / SLOPE) * (slope_c / cos_h)
        for a in range(3):
            unit[s, a] = seps[a] * inv
        return carry

    lax.fori_loop(0, n_slot, geometry, 0)

    mu = lax.broadcasted_iota(jnp.int32, (64, 128), 0).astype(F32) * (
        CENTER_MAX / 63.0 * SCALE
    )
    ones = jnp.ones((16, 256), BF16)
    groups = half // PAIRS

    def place(n):
        return lax.rem(n, n_slot), n // n_slot * PAIRS

    def pair_row(ref, s, row):
        return jnp.concatenate(
            [ref[s, pl.ds(row, 1), :], ref[s, pl.ds(row + PAIRS, 1), :]], axis=1
        )

    def hidden_group(n):
        s, base = place(n)
        for b in range(PAIRS):
            ip = base + b
            x = jnp.concatenate(
                [
                    dist[s, pl.ds(2 * base + b, 1), :] - mu,
                    dist[s, pl.ds(2 * base + b + PAIRS, 1), :] - mu,
                ],
                axis=1,
            )
            wide = jnp.exp2(-(x * x))
            slope_in[s, ip] = (wide * x).astype(BF16)
            g = wide.astype(BF16)
            pre = jnp.dot(
                w1a[:, 0:80], jnp.concatenate([g, ones], axis=0), preferred_element_type=F32
            ).astype(BF16)
            e = jnp.exp2(pre * jnp.asarray(1.0 / LN2, BF16))
            hid[s, ip] = lax.log2(e + jnp.asarray(0.5, BF16))

    def message_group(n):
        s, base = place(n)
        scaled = jnp.concatenate(
            [hid[s, base + b] * row16(pair_row(cm, s, 2 * base + b) * LN2) for b in range(PAIRS)],
            axis=0,
        )
        a = jnp.dot(scaled, diag[s], preferred_element_type=F32)
        w2 = w2f[...]
        for b in range(PAIRS):
            part_a = a[b * 128:(b + 1) * 128]
            msg[s, pl.ds(2 * base + b, 1), :] = jnp.sum(part_a[:, 0:128] * w2, axis=0, keepdims=True)
            msg[s, pl.ds(2 * base + b + PAIRS, 1), :] = jnp.sum(
                part_a[:, 128:256] * w2, axis=0, keepdims=True
            )

    total_groups = n_slot * groups

    def run(first, last, body):
        def step(n, carry):
            body(n)
            return carry
        lax.fori_loop(first, last, step, 0)

    def pass_near(k):
        arrival(near(k))
        twin_copy(k).start()
        hand_near(k).start()

    def pass_far(k):
        arrival(far(k))
        hand_far(k).start()

    def arrive_pair(k):
        arrival(other_core(near(k)))
        arrival(other_core(far(k)))

    run(0, PASS, hidden_group)
    each(n_ring, pass_near)
    run(PASS, HAND, hidden_group)
    every(n_ring, pass_far)
    run(HAND, LAG, hidden_group)
    every(n_ring, arrive_pair)

    def set_diag(s, carry):
        _, c = tiles_of(s)
        p = proj_all[c]
        z = jnp.zeros((128, 128), BF16)
        diag[s, 0:128, 0:128] = p
        diag[s, 0:128, 128:256] = z
        diag[s, 128:256, 0:128] = z
        diag[s, 128:256, 128:256] = p
        q = jnp.transpose(p.astype(F32)).astype(BF16)
        diag_t[s, 0:128, 0:128] = q
        diag_t[s, 0:128, 128:256] = z
        diag_t[s, 128:256, 0:128] = z
        diag_t[s, 128:256, 128:256] = q
        return carry

    lax.fori_loop(0, n_slot, set_diag, 0)

    def both(n):
        message_group(n - LAG)
        hidden_group(n)

    run(LAG, total_groups, both)

    span = 2 * PAIRS

    def part_rows(h):
        return slice(h * span, (h + 1) * span)

    def add_bias(h):
        def body(s, carry):
            weight_sum = jnp.dot(
                cm[s, part_rows(h)].astype(BF16), diag[s, 0:128, 0:128],
                preferred_element_type=F32,
            )
            msg[s, part_rows(h)] = msg[s, part_rows(h)] + weight_sum * b2_ref[...]
            return carry
        lax.fori_loop(0, n_slot, body, 0)

    def gather_part(h):
        def body(tile, carry):
            total = None
            for s in range(n_slot):
                t, _ = tiles_of(s)
                term = msg[s, part_rows(h)] * jnp.where(t == tile, 1.0, 0.0)
                total = term if total is None else total + term
            part[h, tile] = total.astype(BF16)
            return carry
        lax.fori_loop(0, n_col, body, 0)
        msg_in[h, my_col] = part[h, my_col]

    def msg_copy(h, k, tile, src_index):
        return to_col(
            part.at[h, tile], msg_in.at[h, src_index], ms.at[h * n_col + k],
            mr.at[h * n_col + src_index], col_peer(k),
        )

    for h in range(groups):
        run(max(total_groups - LAG, h * n_slot), (h + 1) * n_slot, message_group)
        add_bias(h)
        gather_part(h)
        each(n_col, lambda k, h=h: msg_copy(h, k, col_peer(k), my_col).start())

    def derivative_group(n):
        s, base = place(n)
        for b in range(PAIRS):
            ip = base + b
            slope = jnp.dot(
                w1d[...], slope_in[s, ip], preferred_element_type=F32
            ).astype(BF16)
            level = hid[s, ip]
            sig = jnp.asarray(1.0, BF16) - jnp.exp2(jnp.asarray(-1.0, BF16) - level)
            hid[s, ip] = slope * sig + level * row16(pair_row(ratio, s, 2 * base + b))

    direction = lax.dot_general(
        jnp.broadcast_to(rw_ref[...], (8, 128)), wo2_ref[...].astype(F32),
        (((1,), (1,)), ((), ())), precision=lax.Precision.HIGHEST,
        preferred_element_type=F32,
    )[0:1, :]

    def grad_copy(h, k, src_index):
        return to_col(
            grad_own.at[h], grad_all[h].at[src_index], gs.at[h * n_col + k],
            gr.at[h * n_col + src_index], col_peer(k),
        )

    def atom_update(h):
        each(n_col, lambda k: msg_copy(h, k, col_peer(k), col_peer(k)).wait_recv())
        total = msg_in[h, 0].astype(F32)
        for k in range(1, n_col):
            total = total + msg_in[h, k].astype(F32)
        act_in = jnp.dot(total.astype(BF16), wo1_ref[...], preferred_element_type=F32) + bo1_ref[...]
        small = jnp.exp(-jnp.abs(act_in))
        activated = (jnp.maximum(act_in, 0.0) + jnp.log(1.0 + small) - LN2).astype(BF16)
        sig = jnp.where(act_in >= 0.0, 1.0, small) / (1.0 + small)
        grad_own[h] = lax.dot_general(
            sig * direction, wo1_ref[...].astype(F32), (((1,), (1,)), ((), ())),
            precision=lax.Precision.HIGHEST, preferred_element_type=F32,
        ).astype(BF16)
        grad_all[h][my_col] = grad_own[h]
        each(n_col, lambda k: grad_copy(h, k, my_col).start())
        update[part_rows(h)] = (
            jnp.dot(activated, wo2_ref[...], preferred_element_type=F32) + bo2_ref[...]
        )

    done = 0
    for h in range(groups):
        run(done, SPLITS[h], derivative_group)
        done = SPLITS[h]
        atom_update(h)
    run(done, total_groups, derivative_group)
    fout_ref[...] = (feat_ref[...].astype(F32) + jnp.transpose(update[...])).astype(BF16)

    def spread_grad(h):
        def body(s, carry):
            t, _ = tiles_of(s)
            grad_f[s, part_rows(h)] = grad_all[h][t].astype(F32)
            return carry
        lax.fori_loop(0, n_slot, body, 0)

    def dist_group(n):
        s, base = place(n)
        w2 = w2_ref[...]
        lhs = jnp.concatenate(
            [
                jnp.concatenate(
                    [
                        w2 * row16(grad_f[s, pl.ds(2 * base + b, 1), :]),
                        w2 * row16(grad_f[s, pl.ds(2 * base + b + PAIRS, 1), :]),
                    ],
                    axis=1,
                )
                for b in range(PAIRS)
            ],
            axis=0,
        )
        q = jnp.dot(lhs, diag_t[s], preferred_element_type=F32)
        for b in range(PAIRS):
            product = q[b * 128:(b + 1) * 128].astype(BF16) * hid[s, base + b]
            folded = (product[0:64] + product[64:128]).astype(F32)
            row = jnp.sum(folded, axis=0, keepdims=True)
            dgrad[s, pl.ds(2 * base + b, 1), :] = row[:, 0:128]
            dgrad[s, pl.ds(2 * base + b + PAIRS, 1), :] = row[:, 128:256]

    for h in range(groups):
        each(n_col, lambda k, h=h: grad_copy(h, k, col_peer(k)).wait_recv())
        spread_grad(h)
        run(h * n_slot, (h + 1) * n_slot, dist_group)

    def force_slot(s, carry):
        g_b2 = (grad_f[s] * b2_ref[...]).astype(BF16)
        plain = jnp.dot(g_b2, diag_t[s, 0:128, 0:128], preferred_element_type=F32)
        d = dgrad[s] * (cm[s] * SLOPE) + cpm[s] * plain
        rows, cols = [], []
        for a in range(3):
            push = unit[s, a] * d
            cols.append(jnp.sum(push, axis=0, keepdims=True))
            rows.append(-jnp.sum(jnp.transpose(push), axis=0, keepdims=True))
        pad = [jnp.zeros((5, 128), F32)]
        rforce[s] = jnp.concatenate(rows + pad, axis=0)
        cforce[s] = jnp.concatenate(cols + pad, axis=0)
        return carry

    lax.fori_loop(0, n_slot, force_slot, 0)

    def spread(source, target, which, n):
        def one(tile, carry):
            total = None
            for s in range(n_slot):
                term = source[s] * jnp.where(tiles_of(s)[which] == tile, 1.0, 0.0)
                total = term if total is None else total + term
            target[tile] = total[0:3]
            return carry
        lax.fori_loop(0, n, one, 0)

    spread(cforce, cpart, 1, n_row)
    spread(rforce, rpart, 0, n_col)
    cforce_in[my_row] = cpart[my_row]
    rforce_in[my_col] = rpart[my_col]

    def cforce_copy(k, tile, src_index):
        return to_row(cpart.at[tile], cforce_in.at[src_index], cfs.at[k], cfr.at[src_index], row_peer(k))

    def rforce_copy(k, tile, src_index):
        return to_col(rpart.at[tile], rforce_in.at[src_index], rfs.at[k], rfr.at[src_index], col_peer(k))

    each(n_row, lambda k: cforce_copy(k, row_peer(k), my_row).start())
    each(n_col, lambda k: rforce_copy(k, col_peer(k), my_col).start())

    each(n_row, lambda k: pos_col_copy(k, my_row).wait_send())
    each(n_col, lambda k: pos_row_copy(k, my_col).wait_send())
    each(n_ring, lambda k: ring_copy(k).wait_send())
    every(n_ring, lambda k: twin_copy(k).wait_send())
    every(n_ring, lambda k: hand_near(k).wait_send())
    every(n_ring, lambda k: hand_far(k).wait_send())
    for h in range(groups):
        each(n_col, lambda k, h=h: msg_copy(h, k, col_peer(k), my_col).wait_send())
        each(n_col, lambda k, h=h: grad_copy(h, k, my_col).wait_send())

    each(n_col, lambda k: rforce_copy(k, col_peer(k), col_peer(k)).wait_recv())
    each(n_row, lambda k: cforce_copy(k, row_peer(k), row_peer(k)).wait_recv())
    force = rforce_in[0]
    for k in range(1, n_col):
        force = force + rforce_in[k]
    for k in range(n_row):
        force = force + cforce_in[k]
    force_ref[...] = force
    each(n_row, lambda k: cforce_copy(k, row_peer(k), my_row).wait_send())
    each(n_col, lambda k: rforce_copy(k, col_peer(k), my_col).wait_send())


def solution(mesh):
    n_row, n_col = mesh.shape["row"], mesh.shape["col"]

    def local(features, positions, tile_pairs, pair_count, masks, w_in, w_f1, b_f1, w_f2, b_f2,
              w_o1, b_o1, w_o2, b_o2, read_w):
        n_slot = masks.shape[2]
        vmem = pl.BlockSpec(memory_space=pltpu.VMEM)
        smem = pl.BlockSpec(memory_space=pltpu.SMEM)
        tile = (128, 128)
        dma = pltpu.SemaphoreType.DMA
        return pl.pallas_call(
            functools.partial(kernel, n_row, n_col, n_slot),
            out_shape=(
                jax.ShapeDtypeStruct(features.shape, BF16),
                jax.ShapeDtypeStruct(positions.shape, F32),
            ),
            in_specs=[smem, smem] + [vmem] * 13,
            out_specs=(vmem, vmem),
            scratch_shapes=[
                pltpu.VMEM((n_col, 3, 128), F32),
                pltpu.VMEM((n_row, 3, 128), F32),
                pltpu.VMEM((n_row,) + tile, BF16),
                pltpu.VMEM(tile, BF16),
                pltpu.VMEM((128, 64), BF16),
                pltpu.VMEM(tile, F32),
                pltpu.VMEM((n_slot, 256, 256), BF16),
                pltpu.VMEM((n_slot, 256, 256), BF16),
                pltpu.VMEM((n_slot,) + tile, F32),
                pltpu.VMEM((n_slot,) + tile, F32),
                pltpu.VMEM((n_slot,) + tile, F32),
                pltpu.VMEM((n_slot,) + tile, F32),
                pltpu.VMEM((n_slot, 3) + tile, F32),
                pltpu.VMEM((n_slot, 64, 128, 256), BF16),
                pltpu.VMEM((n_slot, 64, 64, 256), BF16),
                pltpu.VMEM((n_slot,) + tile, F32),
                pltpu.VMEM((64 // PAIRS, n_col, 2 * PAIRS, 128), BF16),
                pltpu.VMEM((64 // PAIRS, n_col, 2 * PAIRS, 128), BF16),
                pltpu.VMEM((64 // PAIRS, 2 * PAIRS, 128), BF16),
                pltpu.VMEM((n_col, 2 * PAIRS, 128), BF16),
                pltpu.VMEM((n_col, 2 * PAIRS, 128), BF16),
                pltpu.VMEM(tile, F32),
                pltpu.VMEM((n_slot,) + tile, F32),
                pltpu.VMEM((n_slot,) + tile, F32),
                pltpu.VMEM((n_slot, 8, 128), F32),
                pltpu.VMEM((n_slot, 8, 128), F32),
                pltpu.VMEM((n_col, 3, 128), F32),
                pltpu.VMEM((n_row, 3, 128), F32),
                pltpu.VMEM((n_col, 3, 128), F32),
                pltpu.VMEM((n_row, 3, 128), F32),
                dma((n_row,)), dma((n_row,)),
                dma((n_col,)), dma((n_col,)),
                dma((n_row // 4,)), dma((n_row // 4,)), dma((n_row // 2,)), dma((n_row,)),
                dma((64 // PAIRS * n_col,)), dma((64 // PAIRS * n_col,)),
                dma((64 // PAIRS * n_col,)), dma((64 // PAIRS * n_col,)),
                dma((n_col,)), dma((n_col,)),
                dma((n_row,)), dma((n_row,)),
            ],
            compiler_params=pltpu.CompilerParams(
                collective_id=0, has_side_effects=True, vmem_limit_bytes=56 << 20
            ),
        )(
            tile_pairs.reshape(tile_pairs.shape[2:]), pair_count, features, positions,
            masks.reshape(masks.shape[2:]),
            w_in, w_f1, b_f1.reshape(1, -1), w_f2, b_f2.reshape(1, -1),
            w_o1, b_o1.reshape(1, -1), w_o2, b_o2.reshape(1, -1), read_w.reshape(1, -1),
        )

    split = P(None, ("row", "col"))
    return jax.shard_map(
        local, mesh=mesh,
        in_specs=(split, split, P("row", "col", None, None), P("row", "col"),
                  P("row", "col", None, None, None)) + (P(),) * 10,
        out_specs=(split, split), check_vma=False,
    )
```
